512 devices in a mesh: member: 4 (over y_lo), space: 128 (over x, y_hi, z, core).
Axes of the slice: x: 4, y: 8 (y_hi: 2, y_lo: 4; y = y_hi * 4 + y_lo), z: 8, core: 2. Of those that a mesh axis runs over, the one named last changes fastest.
Arguments:
- initial_fields: bfloat16 [128, 64, 16384], P('member', None, 'space'), may hold values from -4 to 4
- encode_weight: bfloat16 [64, 256], replicated, may hold values from -0.75 to 0.75
- send_weight: bfloat16 [1, 256, 256], replicated, may hold values from -0.375 to 0.375
- receive_weight: bfloat16 [1, 256, 256], replicated, may hold values from -0.375 to 0.375
- update_weight: bfloat16 [1, 256, 256], replicated, may hold values from -0.375 to 0.375
- norm_gain: bfloat16 [1, 256], replicated, may hold values from 0.099609375 to 1.8984375
- decode_weight: bfloat16 [256, 64], replicated, may hold values from -0.375 to 0.375
- edge_senders: int32 [16384, 4], P('space'), may hold values from 0 to 191
- halo_nodes: int32 [2, 4096], P(None, 'space'), may hold values from 0 to 127, as said below
- observed_perturbation: bfloat16 [512, 128, 256], P(('member', 'space')), may hold values from -2.5 to 2.5
- observed_values: bfloat16 [512, 2, 256], P(('member', 'space')), may hold values from -3.5 to 3.5, as said below
- region_neighbours: int32 [512, 8], P(('member', 'space')), may hold values from 0 to 511, as said below
Outputs:
- analysis: bfloat16 [128, 64, 16384], P('member', None, 'space')
The draws below stay inside these ranges and needn't reach their ends.
Inputs may be any that keep to these rules, and one draw needn't show every extreme that they name: edge_senders[n, k] indexes the list of the 128 nodes of n's space block, followed by the 32 nodes that halo_nodes row 0 names in the block before and the 32 that row 1 names in the block after (blocks wrap around). For each space block b, halo_nodes[0, b * 32 : (b + 1) * 32] are distinct node indices within block b - 1 and halo_nodes[1, ...] distinct ones within block b + 1, taken modulo 128. `region_neighbours`: each row lists 8 distinct regions other than r = a * 128 + b; each is ((a + p) mod 4) * 128 + ((b + s) mod 128) with either p = 0 and 1 <= |s| <= 2, or |p| = 1 and |s| <= 1. `observed_values`: row 0 of each region holds positive inverse error variances of at least 0.25.
All inputs are finite; a program needn't handle non-finite values.
Results may differ from the reference program's by a relative error of at most 0.0059.
Values may be sent and summed in bfloat16 or wider, within the bound.
A program may use at most 64 MiB of HBM per device.

```python
import math
import jax
import jax.numpy as jnp
import numpy as np
from jax import lax

H = 256
VERTEX_FEATURES = 64
NODE_DEV = 128
OBS_REG = 256
LAYERS = 1
ITERS_NS = 5
DEG = 4
NEIGH = 8
MEMBER_TOTAL = 128
NODES = 16384
HALO = 32
AREA_VERTICES = 32
AREA_LATITUDES = 4
AREA_LONGITUDES = 128
AREA_TOTAL = 512


ROW_SHIFTS = np.array([0, 0, 0, 0, -1, -1, -1, 1, 1, 1], np.int32)


COLUMN_SHIFTS = np.array([-2, -1, 1, 2, -1, 0, 1, -1, 0, 1], np.int32)


def draw_initial_fields(key, part):
    first = jax.random.fold_in(key, 0)
    noise = jax.random.normal(first, (MEMBER_TOTAL, VERTEX_FEATURES, NODES), jnp.float32)
    return jnp.clip(noise, -4.0, 4.0).astype(jnp.bfloat16)


def draw_observed_values(key, part):
    first, second = jax.random.split(key)
    lowest = math.log(0.25)
    highest = math.log(3.5)
    inverse_var = jnp.exp(jax.random.uniform(first, (AREA_TOTAL, 1, OBS_REG), jnp.float32, lowest, highest))
    innovation = jax.random.normal(second, (AREA_TOTAL, 1, OBS_REG), jnp.float32)
    innovation = jnp.clip(innovation, -3.5, 3.5)
    return jnp.concatenate([inverse_var, innovation], axis=1).astype(jnp.bfloat16)


def draw_halo_nodes(key, part):
    scores = jax.random.randint(key, (2, AREA_LONGITUDES, NODE_DEV), 0, 65536) * NODE_DEV + jnp.arange(NODE_DEV, dtype=jnp.int32)
    chosen = jnp.argsort(scores, axis=2)
    return chosen[:, :, :HALO].reshape(2, AREA_LONGITUDES * HALO).astype(jnp.int32)


def draw_region_neighbours(key, part):
    scores = jax.random.randint(key, (AREA_TOTAL, 10), 0, 65536) * 16 + jnp.arange(10, dtype=jnp.int32)
    chosen = jnp.argsort(scores, axis=1)[:, :NEIGH]
    region = jnp.arange(AREA_TOTAL, dtype=jnp.int32)[:, None]
    row_index = (region // AREA_LONGITUDES + jnp.asarray(ROW_SHIFTS)[chosen]) % AREA_LATITUDES
    column_index = (region % AREA_LONGITUDES + jnp.asarray(COLUMN_SHIFTS)[chosen]) % AREA_LONGITUDES
    return (row_index * AREA_LONGITUDES + column_index).astype(jnp.int32)


def place_ends(values, rng, least, largest):
    index_at = [jax.random.randint(jax.random.fold_in(rng, axis), (), 0, length) for axis, length in enumerate(values.shape)]
    widest = values.shape.index(max(values.shape))
    next_to = index_at[:widest] + [(index_at[widest] + 1) % values.shape[widest]] + index_at[widest + 1:]
    return values.at[tuple(index_at)].set(least).at[tuple(next_to)].set(largest)


def steps_of(rng, dims, cuts, least, top_value):
    def one(dim, shards_of):
        draws = jax.random.uniform(jax.random.fold_in(jax.random.fold_in(rng, 6), dim), (shards_of,), jnp.float32, least / len(cuts), top_value / len(cuts))
        return jnp.repeat(jnp.exp(draws), dims[dim] // shards_of).reshape((-1,) + (1,) * (len(dims) - dim - 1))

    gain = one(*cuts[0])
    for cut in cuts[1:]:
        gain = gain * one(*cut)
    return gain


def scatter_about(key, shape, width, most, pieces=(), kind=jnp.bfloat16):
    level = steps_of(key, shape, pieces, -0.22, 0.18) if pieces else 1.0
    drawn = jax.random.normal(key, shape, jnp.float32) * width * level
    return jnp.minimum(jnp.maximum(drawn, -most), most).astype(kind)


def setup_inputs(seed: int = 0) -> dict:
    streams_of = jax.random.split(jax.random.key(seed), 13)
    initial_fields = draw_initial_fields(jax.random.fold_in(streams_of[12], 71), 0)
    encode_weight = scatter_about(streams_of[1], (VERTEX_FEATURES, H), VERTEX_FEATURES ** -0.5, 0.75)
    send_weight = scatter_about(streams_of[2], (LAYERS, H, H), H ** -0.5, 0.375)
    receive_weight = scatter_about(streams_of[3], (LAYERS, H, H), H ** -0.5, 0.375)
    update_weight = scatter_about(streams_of[4], (LAYERS, H, H), H ** -0.5, 0.375)
    norm_gain = jnp.clip(1.0 + 0.18 * jax.random.normal(streams_of[5], (LAYERS, H), jnp.float32), 0.099609375, 1.8984375).astype(jnp.bfloat16)
    decode_weight = scatter_about(streams_of[6], (H, VERTEX_FEATURES), H ** -0.5, 0.375)
    edge_senders = place_ends(jax.random.randint(streams_of[7], (NODES, DEG), 0, NODE_DEV + 2 * HALO), jax.random.fold_in(streams_of[7], 1), 0, (NODE_DEV + 2 * HALO) - 1).astype(jnp.int32)
    halo_nodes = draw_halo_nodes(jax.random.fold_in(streams_of[12], 71), 0)
    observed_perturbation = scatter_about(streams_of[9], (AREA_TOTAL, MEMBER_TOTAL, OBS_REG), 0.3, 2.5, ((0, 512),))
    observed_values = draw_observed_values(jax.random.fold_in(streams_of[12], 71), 0)
    region_neighbours = draw_region_neighbours(jax.random.fold_in(streams_of[12], 71), 0)
    return {"initial_fields": initial_fields, "encode_weight": encode_weight, "send_weight": send_weight, "receive_weight": receive_weight, "update_weight": update_weight, "norm_gain": norm_gain, "decode_weight": decode_weight, "edge_senders": edge_senders, "halo_nodes": halo_nodes, "observed_perturbation": observed_perturbation, "observed_values": observed_values, "region_neighbours": region_neighbours}


EPSILON = 1e-05
FULL_PRECISION = lax.Precision.HIGHEST

def wide_dot(left, right):
    return jnp.dot(left.astype(jnp.float32), right.astype(jnp.float32), precision=FULL_PRECISION)

def normalize(messages, gains):
    mean_square = lax.optimization_barrier(jnp.mean(messages * messages, axis=-1, keepdims=True))
    return messages * lax.rsqrt(mean_square + EPSILON) * gains.astype(jnp.float32)

def inverse_root(system):
    extent = system.shape[0]
    identity = jnp.eye(extent, dtype=jnp.float32)
    scaling = jnp.sqrt(jnp.sum(system * system))
    iterate = system / scaling
    inverse = identity
    for _ in range(ITERS_NS):
        correction = 1.5 * identity - 0.5 * jnp.dot(inverse, iterate, precision=FULL_PRECISION)
        iterate = jnp.dot(iterate, correction, precision=FULL_PRECISION)
        inverse = jnp.dot(correction, inverse, precision=FULL_PRECISION)
    return (inverse, scaling)

def analyse(states, gram_matrix, forcing):
    ensemble = states.shape[0]
    identity = jnp.eye(ensemble, dtype=jnp.float32)
    system = identity + gram_matrix / (ensemble - 1)
    inverse, scaling = inverse_root(system)
    inner = jnp.dot(inverse, forcing, precision=FULL_PRECISION)
    mean_weights = jnp.dot(inverse, inner, precision=FULL_PRECISION) / (scaling * (ensemble - 1))
    transform = inverse / jnp.sqrt(scaling) + mean_weights[:, None]
    mean_state = lax.optimization_barrier(jnp.mean(states, axis=0))
    anomalies = states - mean_state
    moved = jnp.einsum('ij,is->js', transform, anomalies, precision=FULL_PRECISION)
    return (mean_state + moved).astype(jnp.bfloat16)

def offsets(neighbours, own_row, own_column, row_count, column_count):
    near_row = (neighbours // column_count - own_row + 1) % row_count - 1
    near_column = (neighbours % column_count - own_column + 2) % column_count - 2
    distance = (near_row * near_row + near_column * near_column).astype(jnp.float32)
    return (near_row, near_column, 1.0 / (1.0 + distance / 2.0))

def reference(initial_fields, encode_weight, send_weight, receive_weight, update_weight, norm_gain, decode_weight, edge_senders, halo_nodes, observed_perturbation, observed_values, region_neighbours):
    block = (jnp.arange(NODES, dtype=jnp.int32) // NODE_DEV)[:, None]
    left_pick = jnp.clip(edge_senders - NODE_DEV, 0, HALO - 1)
    right_pick = jnp.clip(edge_senders - NODE_DEV - HALO, 0, HALO - 1)
    left_node = (block - 1) % AREA_LONGITUDES * NODE_DEV + halo_nodes[0][block * HALO + left_pick]
    right_node = (block + 1) % AREA_LONGITUDES * NODE_DEV + halo_nodes[1][block * HALO + right_pick]
    own_node = block * NODE_DEV + jnp.minimum(edge_senders, NODE_DEV - 1)
    senders = jnp.where(edge_senders < NODE_DEV, own_node, jnp.where(edge_senders < NODE_DEV + HALO, left_node, right_node)).astype(jnp.int32)

    def predicted_replica(present_field):
        stream = wide_dot(present_field.T, encode_weight)
        for layer_index in range(LAYERS):
            rounded = stream.astype(jnp.bfloat16)
            sent = wide_dot(rounded, send_weight[layer_index]).astype(jnp.bfloat16)
            received = wide_dot(rounded, receive_weight[layer_index])
            messages = jnp.zeros_like(received)
            for slot_index in range(DEG):
                picked_rows = sent[senders[:, slot_index]].astype(jnp.float32)
                messages = messages + jax.nn.silu(picked_rows + received)
            normed = normalize(messages, norm_gain[layer_index]).astype(jnp.bfloat16)
            stream = stream + wide_dot(normed, update_weight[layer_index])
        field_change = wide_dot(stream.astype(jnp.bfloat16), decode_weight)
        return (present_field.astype(jnp.float32) + field_change.T).astype(jnp.bfloat16)
    predicted_fields = lax.map(predicted_replica, initial_fields)
    domain_pieces = predicted_fields.reshape(MEMBER_TOTAL, VERTEX_FEATURES, AREA_LONGITUDES, AREA_LATITUDES, AREA_VERTICES).transpose(3, 2, 0, 1, 4).reshape(AREA_TOTAL, MEMBER_TOTAL, VERTEX_FEATURES * AREA_VERTICES)

    def region_step(inputs):
        states, region, neighbours = inputs
        _, _, weights = offsets(neighbours, region // AREA_LONGITUDES, region % AREA_LONGITUDES, AREA_LATITUDES, AREA_LONGITUDES)
        chosen = jnp.concatenate([region[None], neighbours]).astype(jnp.int32)
        all_weights = jnp.concatenate([jnp.ones((1,), jnp.float32), weights])
        perturbation = observed_perturbation[chosen].astype(jnp.float32)
        values = observed_values[chosen].astype(jnp.float32)
        partial_grams = jnp.einsum('kio,kjo->kij', perturbation * values[:, 0][:, None, :], perturbation, precision=FULL_PRECISION)
        gram_matrix = jnp.einsum('k,kij->ij', all_weights, partial_grams, precision=FULL_PRECISION)
        partial_forcing = jnp.einsum('kio,ko->ki', perturbation, values[:, 0] * values[:, 1], precision=FULL_PRECISION)
        forcing = jnp.dot(all_weights, partial_forcing, precision=FULL_PRECISION)
        return analyse(states.astype(jnp.float32), gram_matrix, forcing)
    analysed = lax.map(region_step, (domain_pieces, jnp.arange(AREA_TOTAL, dtype=jnp.int32), region_neighbours))
    return analysed.reshape(AREA_LATITUDES, AREA_LONGITUDES, MEMBER_TOTAL, VERTEX_FEATURES, AREA_VERTICES).transpose(2, 3, 1, 0, 4).reshape(MEMBER_TOTAL, VERTEX_FEATURES, NODES)
```

```python
import functools

import jax
import jax.numpy as jnp
from jax import lax
from jax.experimental import pallas as pl
from jax.experimental.pallas import tpu as pltpu
from jax.sharding import PartitionSpec as P

ITERS_NS = 5
EPSILON = 1e-05
FULL_PRECISION = lax.Precision.HIGHEST
MESH = pl.DeviceIdType.MESH
BF16 = jnp.bfloat16
F32 = jnp.float32

MEMBERS = 32
CHANNELS = 64
NODES = 128
HIDDEN = 256
HALO = 32
SLOTS = 4
PARTS = 4
ENSEMBLE = 128
GRAM_ROWS = 144
MEMBER_CHUNKS = 2
CHANNEL_CHUNKS = 4


def dot(left, right):
    return jnp.dot(left, right, preferred_element_type=F32)


def dot_nt(left, right):
    return lax.dot_general(left, right, (((1,), (1,)), ((), ())), preferred_element_type=F32)


def iota(shape, dim):
    return lax.broadcasted_iota(jnp.int32, shape, dim)


def eye(extent, dtype):
    return jnp.where(iota((extent, extent), 0) == iota((extent, extent), 1), 1.0, 0.0).astype(dtype)


def split(values):
    high = values.astype(BF16)
    return high, (values - high.astype(F32)).astype(BF16)


def kernel(
    member_count,
    space_count,
    fields_hbm,
    we_ref,
    ws_ref,
    wr_ref,
    wu_ref,
    gain_ref,
    wd_ref,
    edge_ref,
    halo_ref,
    pert_ref,
    vals_ref,
    near_ref,
    out_ref,
    fv,
    we_t,
    wsr_t,
    wu_t,
    wd_t,
    gain_col,
    pick,
    perm,
    perm_halo,
    lists,
    nears,
    halo_send,
    halo_recv,
    se,
    rv,
    sh,
    vs,
    ms,
    nb,
    fs,
    sb,
    xr,
    zs,
    zr,
    os_,
    gram_own,
    gram_send,
    gram_member,
    sum_send,
    sum_recv,
    gram_far,
    field_sem,
    list_send_sem,
    list_recv_sem,
    near_send_sem,
    near_recv_sem,
    halo_send_sem,
    halo_recv_sem,
    gm_send_sem,
    gm_recv_sem,
    sum_send_sem,
    sum_recv_sem,
    far_send_sem,
    far_recv_sem,
    x_send_sem,
    x_recv_sem,
    z_send_sem,
    z_recv_sem,
):
    row = lax.axis_index("member")
    column = lax.axis_index("space")

    def at_member(offset):
        return (lax.rem(row + offset + member_count, member_count), column)

    def at_space(offset):
        return (row, lax.rem(column + offset + space_count, space_count))

    def remote(source, target, send_sem, recv_sem, device):
        return pltpu.make_async_remote_copy(
            src_ref=source,
            dst_ref=target,
            send_sem=send_sem,
            recv_sem=recv_sem,
            device_id=device,
            device_id_type=MESH,
        )

    load_fields = pltpu.make_async_copy(fields_hbm, fv, field_sem)
    load_fields.start()
    barrier = pltpu.get_barrier_semaphore()
    partners = [at_space(-1), at_space(1), at_space(-2), at_space(2)]
    partners += [at_member(d) for d in range(1, PARTS)]
    for partner in partners:
        pl.semaphore_signal(barrier, inc=1, device_id=partner, device_id_type=MESH)

    pert = pert_ref[0]
    variance = vals_ref[0, 0:1, :].astype(F32)
    innovation = vals_ref[0, 1:2, :].astype(F32)
    scaled_high, scaled_low = split(pert.astype(F32) * variance)
    gram = dot_nt(scaled_high, pert) + dot_nt(scaled_low, pert)
    force_high, force_low = split(variance * innovation)
    sub = iota((16, HIDDEN), 0)
    force_rows = jnp.where(
        sub == 0,
        jnp.broadcast_to(force_high.astype(F32), (16, HIDDEN)),
        jnp.where(sub == 1, jnp.broadcast_to(force_low.astype(F32), (16, HIDDEN)), 0.0),
    ).astype(BF16)
    forcing = jnp.sum(dot_nt(force_rows, pert), axis=0, keepdims=True)
    sub16 = iota((16, ENSEMBLE), 0)

    def forcing_rows(values):
        high = values.astype(BF16).astype(F32)
        low = values - high
        return jnp.where(
            sub16 == 0,
            jnp.broadcast_to(high, (16, ENSEMBLE)),
            jnp.where(sub16 == 1, jnp.broadcast_to(low, (16, ENSEMBLE)), 0.0),
        )

    gram_own[0:ENSEMBLE, :] = gram
    gram_own[ENSEMBLE:GRAM_ROWS, :] = forcing_rows(forcing)
    gram_send[...] = gram_own[...].astype(BF16)

    pl.semaphore_wait(barrier, len(partners))

    list_copies = []
    for i, offset in enumerate((1, -1)):
        list_copies.append(
            remote(halo_ref, lists.at[i], list_send_sem.at[i], list_recv_sem.at[i], at_space(offset))
        )
        list_copies.append(
            remote(near_ref, nears.at[i], near_send_sem.at[i], near_recv_sem.at[i], at_space(offset))
        )
    for copy in list_copies:
        copy.start()
    member_copies = [
        remote(gram_send, gram_member.at[i], gm_send_sem.at[i], gm_recv_sem.at[i], at_member(offset))
        for i, offset in enumerate((1, -1))
    ]
    far_copies = [
        remote(gram_send, gram_far.at[i], far_send_sem.at[i], far_recv_sem.at[i], at_space(offset))
        for i, offset in enumerate((2, -2))
    ]
    for copy in member_copies:
        copy.start()

    eye_hidden = eye(HIDDEN, BF16)
    we_t[...] = dot_nt(eye_hidden, we_ref[...]).astype(BF16)
    wsr_t[0:HIDDEN, :] = dot_nt(eye_hidden, ws_ref[0]).astype(BF16)
    wsr_t[HIDDEN:, :] = (dot_nt(eye_hidden, wr_ref[0]) * 0.5).astype(BF16)

    load_fields.wait()
    for i in range(2):
        list_copies[2 * i].wait_recv()

    repeat = jnp.where(
        iota((HALO, NODES), 0) == (iota((HALO, NODES), 1) & (HALO - 1)), 1.0, 0.0
    ).astype(BF16)
    node = iota((NODES, HALO), 0)
    block = iota((NODES, NODES), 1) >> 5
    wanted = []
    for names in (lists[1, 0:1, :], lists[0, 1:2, :]):
        one_hot = jnp.where(node == jnp.broadcast_to(names, (NODES, HALO)), 1.0, 0.0).astype(BF16)
        wanted.append(dot(one_hot, repeat))
    chooser = jnp.concatenate(
        [
            jnp.concatenate([jnp.where(block == q, w, 0.0) for w in wanted], axis=1)
            for q in range(PARTS)
        ],
        axis=0,
    ).astype(BF16)
    groups = MEMBERS // PARTS
    quads = jnp.concatenate(
        [
            jnp.concatenate([fv[PARTS * g + q] for g in range(groups)], axis=0)
            for q in range(PARTS)
        ],
        axis=1,
    )
    chosen = dot(quads, chooser).astype(BF16)
    halo_send[0] = chosen[:, 0:NODES]
    halo_send[1] = chosen[:, NODES:]
    halo_copies = [
        remote(
            halo_send.at[i],
            halo_recv.at[i],
            halo_send_sem.at[i],
            halo_recv_sem.at[i],
            at_space(offset),
        )
        for i, offset in enumerate((1, -1))
    ]
    for copy in halo_copies:
        copy.start()
    for copy in far_copies:
        copy.start()

    def project(g, carry):
        wide = jnp.concatenate([fv[PARTS * g + q] for q in range(PARTS)], axis=1)
        rounded = dot(we_t[...], wide).astype(BF16)
        both = dot(wsr_t[...], rounded)
        for q in range(PARTS):
            se[PARTS * g + q] = both[0:HIDDEN, NODES * q : NODES * (q + 1)].astype(BF16)
            rv[PARTS * g + q] = both[HIDDEN:, NODES * q : NODES * (q + 1)]
        return carry

    lax.fori_loop(0, groups, project, 0)

    wu_t[...] = dot_nt(eye_hidden, wu_ref[0]).astype(BF16)
    wd_t[...] = dot_nt(eye(CHANNELS, BF16), wd_ref[...]).astype(BF16)
    gain_col[...] = dot_nt(eye_hidden, jnp.broadcast_to(gain_ref[...], (NODES, HIDDEN)))
    lane = iota((NODES, HIDDEN), 1)
    for k in range(SLOTS):
        sender = jnp.broadcast_to(edge_ref[:, k : k + 1], (NODES, HIDDEN))
        for i in range(2):
            moved = sender + jnp.where(sender >= NODES, 2 * HALO * i, 0)
            hot = jnp.where(lane == moved, 0.5, 0.0).astype(BF16)
            pick[i, :, NODES * k : NODES * (k + 1)] = dot_nt(eye_hidden, hot).astype(BF16)
    wide_lanes = PARTS * NODES
    r0 = iota((wide_lanes, wide_lanes), 0)
    goal = ((r0 >> 5) & 3) * NODES + (r0 >> 7) * HALO + (r0 & 31)
    perm[...] = jnp.where(iota((wide_lanes, wide_lanes), 1) == goal, 1.0, 0.0).astype(BF16)
    r1 = iota((HIDDEN, HIDDEN), 0)
    goal = ((r1 >> 5) & 3) * (2 * HALO) + (r1 >> 7) * HALO + (r1 & 31)
    perm_halo[...] = jnp.where(iota((HIDDEN, HIDDEN), 1) == goal, 1.0, 0.0).astype(BF16)

    def region(p, s):
        r = lax.rem(row + p + member_count, member_count)
        c = lax.rem(column + s + space_count, space_count)
        return r * space_count + c

    def weight(names, p, s, base):
        held = jnp.sum(
            jnp.where(names == region(p, base + s), 1.0, 0.0), axis=1, keepdims=True
        )
        return held * (1.0 / (1.0 + (p * p + s * s) / 2.0))

    for copy in member_copies:
        copy.wait_recv()
    for i in range(2):
        list_copies[2 * i + 1].wait_recv()
    rows = [(-1, gram_member[0].astype(F32)), (0, gram_own[...]), (1, gram_member[1].astype(F32))]
    for i, (offset, s) in enumerate(((1, -1), (-1, 1))):
        names = nears[1 - i]
        total = sum(weight(names, p, s, offset) * values for p, values in rows)
        sum_send[i, 0:ENSEMBLE, :] = total[0:ENSEMBLE].astype(BF16)
        sum_send[i, ENSEMBLE:, :] = forcing_rows(
            jnp.sum(total[ENSEMBLE:], axis=0, keepdims=True)
        ).astype(BF16)
    sum_copies = [
        remote(
            sum_send.at[i], sum_recv.at[i], sum_send_sem.at[i], sum_recv_sem.at[i], at_space(offset)
        )
        for i, offset in enumerate((1, -1))
    ]
    for copy in sum_copies:
        copy.start()

    for copy in halo_copies:
        copy.wait_recv()

    def project_halo(g, carry):
        at = pl.ds(pl.multiple_of(g * CHANNELS, CHANNELS), CHANNELS)
        both = jnp.concatenate([halo_recv[0, at, :], halo_recv[1, at, :]], axis=1)
        ordered = dot(both, perm_halo[...]).astype(BF16)
        rounded = dot(we_t[...], ordered).astype(BF16)
        values = dot(wsr_t[0:HIDDEN, :], rounded).astype(BF16)
        sh[2 * g] = values[:, 0:NODES]
        sh[2 * g + 1] = values[:, NODES:]
        return carry

    lax.fori_loop(0, groups, project_halo, 0)

    strip = 64

    def forecast(g, place):
        for i in range(2):
            left = jnp.concatenate(
                [
                    jnp.concatenate([se[PARTS * g + 2 * j + i], sh[2 * g + j]], axis=1)
                    for j in range(2)
                ],
                axis=0,
            )
            vs[...] = dot(left, pick[i])
            for j in range(2):
                square = jnp.zeros((8, NODES), F32)
                for top in range(0, HIDDEN, strip):
                    base = rv[PARTS * g + 2 * j + i, top : top + strip, :]
                    total = None
                    for k in range(SLOTS):
                        half = (
                            vs[
                                HIDDEN * j + top : HIDDEN * j + top + strip,
                                NODES * k : NODES * (k + 1),
                            ]
                            + base
                        )
                        term = half + half * jnp.tanh(half)
                        total = term if total is None else total + term
                    ms[top : top + strip, :] = total
                    squared = total * total
                    for t in range(0, strip, 8):
                        square = square + squared[t : t + 8]
                mean_square = jnp.sum(square, axis=0, keepdims=True) * (1.0 / HIDDEN)
                scale = lax.rsqrt(mean_square + EPSILON)
                q = 2 * j + i
                for top in range(0, HIDDEN, strip):
                    nb[top : top + strip, NODES * q : NODES * (q + 1)] = (
                        ms[top : top + strip, :] * scale * gain_col[top : top + strip, :]
                    ).astype(BF16)
        wide = jnp.concatenate([fv[PARTS * g + q] for q in range(PARTS)], axis=1)
        final = (dot(we_t[...], wide) + dot(wu_t[...], nb[...])).astype(BF16)
        values = dot(wd_t[...], final) + wide.astype(F32)
        for q in range(PARTS):
            fs[pl.ds(pl.multiple_of((place * PARTS + q) * CHANNELS, CHANNELS), CHANNELS), :] = (
                values[:, NODES * q : NODES * (q + 1)]
            )

    members = MEMBERS // MEMBER_CHUNKS
    x_copies = []
    for chunk in range(MEMBER_CHUNKS):
        steps = groups // MEMBER_CHUNKS

        def step(place, carry):
            forecast(chunk * steps + place, place)
            return carry

        lax.fori_loop(0, steps, step, 0)
        packed = jnp.concatenate(
            [
                jnp.concatenate(
                    [
                        fs[pl.ds(PARTS * cg + c, members, stride=CHANNELS), :]
                        for c in range(PARTS)
                    ],
                    axis=1,
                ).astype(BF16)
                for cg in range(CHANNELS // PARTS)
            ],
            axis=0,
        )
        turned = dot(packed, perm[...]).astype(BF16)
        for target in range(PARTS):
            sb[target, chunk] = turned[:, NODES * target : NODES * (target + 1)]
        for d in range(1, PARTS):
            device = at_member(d)
            copy = remote(
                sb.at[device[0], chunk],
                xr.at[row, chunk],
                x_send_sem.at[chunk, d - 1],
                x_recv_sem.at[chunk, d - 1],
                device,
            )
            copy.start()
            x_copies.append(copy)
        xr[row, chunk] = sb[row, chunk]

    for copy in sum_copies + far_copies:
        copy.wait_recv()
    names = near_ref[...]
    total = gram_own[...] + sum_recv[0].astype(F32) + sum_recv[1].astype(F32)
    for values, p, s in (
        (gram_member[0], -1, 0),
        (gram_member[1], 1, 0),
        (gram_far[0], 0, -2),
        (gram_far[1], 0, 2),
    ):
        total = total + weight(names, p, s, 0) * values.astype(F32)
    forcing = jnp.sum(total[ENSEMBLE:], axis=0, keepdims=True)
    identity = eye(ENSEMBLE, F32)
    system = identity + total[0:ENSEMBLE] / (ENSEMBLE - 1)
    norm = jnp.sum(jnp.sum(system * system, axis=1, keepdims=True), axis=0, keepdims=True)
    scaling = jnp.sqrt(norm)
    iterate = system / scaling
    inverse = identity

    def full(left, right):
        return jnp.dot(left, right, precision=FULL_PRECISION, preferred_element_type=F32)

    for _ in range(ITERS_NS):
        correction = 1.5 * identity - 0.5 * full(inverse, iterate)
        iterate = full(iterate, correction)
        inverse = full(correction, inverse)
    forcing = jnp.broadcast_to(forcing, (8, ENSEMBLE))
    mean_weights = full(full(forcing, inverse), inverse)[0:1] / (scaling * (ENSEMBLE - 1))
    root = inverse / jnp.sqrt(scaling)
    rest = (
        1.0
        - jnp.sum(root, axis=1, keepdims=True)
        - jnp.sum(mean_weights, axis=1, keepdims=True)
    ) * (1.0 / ENSEMBLE)
    mix_high, mix_low = split(root + mean_weights + rest)

    for copy in x_copies:
        copy.wait_recv()
    per_chunk = CHANNELS // PARTS // CHANNEL_CHUNKS
    owned = MEMBERS
    z_copies = []
    for ch in range(CHANNEL_CHUNKS):
        states = jnp.concatenate(
            [
                jnp.concatenate(
                    [
                        xr[source, chunk, members * cg : members * (cg + 1), :]
                        for source in range(PARTS)
                        for chunk in range(MEMBER_CHUNKS)
                    ],
                    axis=0,
                )
                for cg in range(ch * per_chunk, (ch + 1) * per_chunk)
            ],
            axis=1,
        )
        mixed = (dot(mix_high, states) + dot(mix_low, states)).astype(BF16)
        for target in range(PARTS):
            for cg in range(per_chunk):
                zs[target, ch, owned * cg : owned * (cg + 1), :] = mixed[
                    owned * target : owned * (target + 1), NODES * cg : NODES * (cg + 1)
                ]
        sent = []
        for d in range(1, PARTS):
            device = at_member(d)
            copy = remote(
                zs.at[device[0], ch],
                zr.at[row, ch],
                z_send_sem.at[ch, d - 1],
                z_recv_sem.at[ch, d - 1],
                device,
            )
            copy.start()
            sent.append(copy)
        z_copies.append(sent)
        zr[row, ch] = zs[row, ch]

    span = PARTS * per_chunk
    for ch in range(CHANNEL_CHUNKS):
        for copy in z_copies[ch]:
            copy.wait_recv()
        packed = jnp.concatenate([zr[source, ch] for source in range(PARTS)], axis=1)
        turned = dot(packed, perm[...])
        for cg in range(per_chunk):
            for c in range(PARTS):
                os_[pl.ds(PARTS * cg + c, owned, stride=span), :] = turned[
                    owned * cg : owned * (cg + 1), NODES * c : NODES * (c + 1)
                ]
        for j in range(owned):
            out_ref[j, span * ch : span * (ch + 1), :] = os_[span * j : span * (j + 1), :].astype(
                BF16
            )

    for copy in list_copies + member_copies + far_copies + halo_copies + sum_copies + x_copies:
        copy.wait_send()
    for sent in z_copies:
        for copy in sent:
            copy.wait_send()


def body(*arrays):
    vmem = pl.BlockSpec(memory_space=pltpu.VMEM)
    dma = pltpu.SemaphoreType.DMA
    return pl.pallas_call(
        functools.partial(kernel, lax.axis_size("member"), lax.axis_size("space")),
        out_shape=jax.ShapeDtypeStruct((MEMBERS, CHANNELS, NODES), BF16),
        in_specs=[pl.BlockSpec(memory_space=pl.ANY)] + [vmem] * 11,
        out_specs=vmem,
        scratch_shapes=[
            pltpu.VMEM((MEMBERS, CHANNELS, NODES), BF16),
            pltpu.VMEM((HIDDEN, CHANNELS), BF16),
            pltpu.VMEM((2 * HIDDEN, HIDDEN), BF16),
            pltpu.VMEM((HIDDEN, HIDDEN), BF16),
            pltpu.VMEM((CHANNELS, HIDDEN), BF16),
            pltpu.VMEM((HIDDEN, NODES), F32),
            pltpu.VMEM((2, HIDDEN, SLOTS * NODES), BF16),
            pltpu.VMEM((PARTS * NODES, PARTS * NODES), BF16),
            pltpu.VMEM((HIDDEN, HIDDEN), BF16),
            pltpu.VMEM((2, 2, HALO), jnp.int32),
            pltpu.VMEM((2, 1, 8), jnp.int32),
            pltpu.VMEM((2, MEMBERS // PARTS * CHANNELS, NODES), BF16),
            pltpu.VMEM((2, MEMBERS // PARTS * CHANNELS, NODES), BF16),
            pltpu.VMEM((MEMBERS, HIDDEN, NODES), BF16),
            pltpu.VMEM((MEMBERS, HIDDEN, NODES), F32),
            pltpu.VMEM((MEMBERS // 2, HIDDEN, NODES), BF16),
            pltpu.VMEM((2 * HIDDEN, SLOTS * NODES), F32),
            pltpu.VMEM((HIDDEN, NODES), F32),
            pltpu.VMEM((HIDDEN, PARTS * NODES), BF16),
            pltpu.VMEM((MEMBERS // MEMBER_CHUNKS * CHANNELS, NODES), F32),
            pltpu.VMEM((PARTS, MEMBER_CHUNKS, 256, NODES), BF16),
            pltpu.VMEM((PARTS, MEMBER_CHUNKS, 256, NODES), BF16),
            pltpu.VMEM((PARTS, CHANNEL_CHUNKS, 512 // CHANNEL_CHUNKS, NODES), BF16),
            pltpu.VMEM((PARTS, CHANNEL_CHUNKS, 512 // CHANNEL_CHUNKS, NODES), BF16),
            pltpu.VMEM((MEMBERS * CHANNELS // CHANNEL_CHUNKS, NODES), F32),
            pltpu.VMEM((GRAM_ROWS, ENSEMBLE), F32),
            pltpu.VMEM((GRAM_ROWS, ENSEMBLE), BF16),
            pltpu.VMEM((2, GRAM_ROWS, ENSEMBLE), BF16),
            pltpu.VMEM((2, GRAM_ROWS, ENSEMBLE), BF16),
            pltpu.VMEM((2, GRAM_ROWS, ENSEMBLE), BF16),
            pltpu.VMEM((2, GRAM_ROWS, ENSEMBLE), BF16),
            dma,
            dma((2,)),
            dma((2,)),
            dma((2,)),
            dma((2,)),
            dma((2,)),
            dma((2,)),
            dma((2,)),
            dma((2,)),
            dma((2,)),
            dma((2,)),
            dma((2,)),
            dma((2,)),
            dma((MEMBER_CHUNKS, PARTS - 1)),
            dma((MEMBER_CHUNKS, PARTS - 1)),
            dma((CHANNEL_CHUNKS, PARTS - 1)),
            dma((CHANNEL_CHUNKS, PARTS - 1)),
        ],
        compiler_params=pltpu.CompilerParams(collective_id=0, has_side_effects=True),
        name="cycle",
    )(*arrays)


def solution(mesh):
    placed = (
        P("member", None, "space"),
        P(),
        P(),
        P(),
        P(),
        P(),
        P(),
        P("space", None),
        P(None, "space"),
        P(("member", "space"), None, None),
        P(("member", "space"), None, None),
        P(("member", "space"), None),
    )
    return jax.shard_map(
        body, mesh=mesh, in_specs=placed, out_specs=P("member", None, "space"), check_vma=False
    )
```

```python
import functools

import jax
import jax.numpy as jnp
from jax import lax
from jax.experimental import pallas as pl
from jax.experimental.pallas import tpu as pltpu
from jax.sharding import PartitionSpec as P

ITERS_NS = 5
EPSILON = 1e-05
FULL_PRECISION = lax.Precision.HIGHEST
MESH = pl.DeviceIdType.MESH
BF16 = jnp.bfloat16
F32 = jnp.float32

MEMBERS = 32
CHANNELS = 64
NODES = 128
HIDDEN = 256
HALO = 32
SLOTS = 4
PARTS = 4
ENSEMBLE = 128
GRAM_ROWS = 144
MEMBER_CHUNKS = 4
CHANNEL_CHUNKS = 4
HALO_STEP = 8
OWN_STEP = 16


def dot(left, right):
    return jnp.dot(left, right, preferred_element_type=F32)


def dot_nt(left, right):
    return lax.dot_general(left, right, (((1,), (1,)), ((), ())), preferred_element_type=F32)


def iota(shape, dim):
    return lax.broadcasted_iota(jnp.int32, shape, dim)


def eye(extent, dtype):
    return jnp.where(iota((extent, extent), 0) == iota((extent, extent), 1), 1.0, 0.0).astype(dtype)


def split(values):
    high = values.astype(BF16)
    return high, (values - high.astype(F32)).astype(BF16)


def kernel(
    member_count,
    space_count,
    fields_hbm,
    we_hbm,
    ws_hbm,
    wr_hbm,
    wu_hbm,
    gain_hbm,
    wd_hbm,
    edge_hbm,
    halo_hbm,
    pert_hbm,
    vals_hbm,
    near_hbm,
    out_ref,
    fv,
    we_ref,
    ws_ref,
    wr_ref,
    wu_ref,
    gain_ref,
    wd_t,
    edge_ref,
    halo_ref,
    pert_ref,
    vals_ref,
    near_ref,
    we_t,
    wsr_t,
    wu_t,
    gain_col,
    pick,
    perm,
    perm_halo,
    lists,
    nears,
    halo_send,
    halo_recv,
    se,
    rv,
    sh,
    vs,
    ms,
    nb,
    fs,
    sb,
    xr,
    zs,
    zr,
    os_,
    gram_own,
    gram_send,
    gram_member,
    sum_send,
    sum_recv,
    gram_far,
    load_sem,
    list_send_sem,
    list_recv_sem,
    near_send_sem,
    near_recv_sem,
    halo_send_sem,
    halo_recv_sem,
    gm_send_sem,
    gm_recv_sem,
    sum_send_sem,
    sum_recv_sem,
    far_send_sem,
    far_recv_sem,
    x_send_sem,
    x_recv_sem,
    z_send_sem,
    z_recv_sem,
):
    row = lax.axis_index("member")
    column = lax.axis_index("space")

    def at_member(offset):
        return (lax.rem(row + offset + member_count, member_count), column)

    def at_space(offset):
        return (row, lax.rem(column + offset + space_count, space_count))

    def remote(source, target, send_sem, recv_sem, device):
        return pltpu.make_async_remote_copy(
            src_ref=source,
            dst_ref=target,
            send_sem=send_sem,
            recv_sem=recv_sem,
            device_id=device,
            device_id_type=MESH,
        )

    barrier = pltpu.get_barrier_semaphore()
    partners = [at_space(-1), at_space(1), at_space(-2), at_space(2)]
    partners += [at_member(d) for d in range(1, PARTS)]
    for partner in partners:
        pl.semaphore_signal(barrier, inc=1, device_id=partner, device_id_type=MESH)

    sources = (halo_hbm, near_hbm, pert_hbm, vals_hbm, we_hbm, ws_hbm, wr_hbm, fields_hbm)
    sources += (edge_hbm, wu_hbm, gain_hbm, wd_hbm)
    targets = (halo_ref, near_ref, pert_ref, vals_ref, we_ref, ws_ref, wr_ref, fv)
    targets += (edge_ref, wu_ref, gain_ref, wd_t)
    loads = [
        pltpu.make_async_copy(source, target, load_sem.at[i])
        for i, (source, target) in enumerate(zip(sources, targets))
    ]
    for load in loads:
        load.start()

    eye_hidden = eye(HIDDEN, BF16)
    r1 = iota((HIDDEN, HIDDEN), 0)
    goal = ((r1 >> 5) & 3) * (2 * HALO) + (r1 >> 7) * HALO + (r1 & 31)
    perm_halo[...] = jnp.where(iota((HIDDEN, HIDDEN), 1) == goal, 1.0, 0.0).astype(BF16)
    repeat = jnp.where(
        iota((HALO, NODES), 0) == (iota((HALO, NODES), 1) & (HALO - 1)), 1.0, 0.0
    ).astype(BF16)

    for load in loads[0:4]:
        load.wait()
    pert = pert_ref[0]
    variance = vals_ref[0, 0:1, :].astype(F32)
    innovation = vals_ref[0, 1:2, :].astype(F32)
    scaled_high, scaled_low = split(pert.astype(F32) * variance)
    gram = dot_nt(scaled_high, pert) + dot_nt(scaled_low, pert)
    force_high, force_low = split(variance * innovation)
    sub = iota((16, HIDDEN), 0)
    force_rows = jnp.where(
        sub == 0,
        jnp.broadcast_to(force_high.astype(F32), (16, HIDDEN)),
        jnp.where(sub == 1, jnp.broadcast_to(force_low.astype(F32), (16, HIDDEN)), 0.0),
    ).astype(BF16)
    forcing = jnp.sum(dot_nt(force_rows, pert), axis=0, keepdims=True)
    sub16 = iota((16, ENSEMBLE), 0)

    def forcing_rows(values):
        high = values.astype(BF16).astype(F32)
        low = values - high
        return jnp.where(
            sub16 == 0,
            jnp.broadcast_to(high, (16, ENSEMBLE)),
            jnp.where(sub16 == 1, jnp.broadcast_to(low, (16, ENSEMBLE)), 0.0),
        )

    gram_own[0:ENSEMBLE, :] = gram
    gram_own[ENSEMBLE:GRAM_ROWS, :] = forcing_rows(forcing)
    gram_send[...] = gram_own[...].astype(BF16)

    pl.semaphore_wait(barrier, len(partners))

    list_copies = []
    for i, offset in enumerate((1, -1)):
        list_copies.append(
            remote(halo_ref, lists.at[i], list_send_sem.at[i], list_recv_sem.at[i], at_space(offset))
        )
        list_copies.append(
            remote(near_ref, nears.at[i], near_send_sem.at[i], near_recv_sem.at[i], at_space(offset))
        )
    for copy in list_copies:
        copy.start()
    member_copies = [
        remote(gram_send, gram_member.at[i], gm_send_sem.at[i], gm_recv_sem.at[i], at_member(offset))
        for i, offset in enumerate((1, -1))
    ]
    far_copies = [
        remote(gram_send, gram_far.at[i], far_send_sem.at[i], far_recv_sem.at[i], at_space(offset))
        for i, offset in enumerate((2, -2))
    ]
    for copy in member_copies:
        copy.start()

    for load in loads[4:]:
        load.wait()
    we_t[...] = dot_nt(eye_hidden, we_ref[...]).astype(BF16)
    wsr_t[0:HIDDEN, :] = dot_nt(eye_hidden, ws_ref[0]).astype(BF16)
    wsr_t[HIDDEN:, :] = (dot_nt(eye_hidden, wr_ref[0]) * 0.5).astype(BF16)

    for i in range(2):
        list_copies[2 * i].wait_recv()

    node = iota((NODES, HALO), 0)
    block = iota((NODES, NODES), 1) >> 5
    wanted = []
    for names in (lists[1, 0:1, :], lists[0, 1:2, :]):
        one_hot = jnp.where(node == jnp.broadcast_to(names, (NODES, HALO)), 1.0, 0.0).astype(BF16)
        wanted.append(dot(one_hot, repeat))
    chooser = jnp.concatenate(
        [
            jnp.concatenate([jnp.where(block == q, w, 0.0) for w in wanted], axis=1)
            for q in range(PARTS)
        ],
        axis=0,
    ).astype(BF16)
    groups = MEMBERS // PARTS
    quads = jnp.concatenate(
        [
            jnp.concatenate([fv[PARTS * g + q] for g in range(groups)], axis=0)
            for q in range(PARTS)
        ],
        axis=1,
    )
    chosen = dot(quads, chooser).astype(BF16)
    halo_send[0] = chosen[:, 0:NODES]
    halo_send[1] = chosen[:, NODES:]
    halo_copies = [
        remote(
            halo_send.at[i],
            halo_recv.at[i],
            halo_send_sem.at[i],
            halo_recv_sem.at[i],
            at_space(offset),
        )
        for i, offset in enumerate((1, -1))
    ]
    for copy in halo_copies:
        copy.start()
    for copy in far_copies:
        copy.start()

    for m in range(0, MEMBERS, OWN_STEP):
        wide = jnp.concatenate([fv[m + t] for t in range(OWN_STEP)], axis=1)
        rounded = dot(we_t[...], wide).astype(BF16)
        both = dot(wsr_t[...], rounded)
        for t in range(OWN_STEP):
            se[m + t] = both[0:HIDDEN, NODES * t : NODES * (t + 1)].astype(BF16)
            rv[m + t] = both[HIDDEN:, NODES * t : NODES * (t + 1)]

    wu_t[...] = dot_nt(eye_hidden, wu_ref[0]).astype(BF16)
    gain_col[...] = dot_nt(eye_hidden, jnp.broadcast_to(gain_ref[...], (NODES, HIDDEN)))
    tall = iota((HIDDEN, NODES), 0)
    for k in range(SLOTS):
        sender = jnp.broadcast_to(edge_ref[k : k + 1, :], (HIDDEN, NODES))
        for i in range(2):
            moved = sender + jnp.where(sender >= NODES, 2 * HALO * i, 0)
            hot = jnp.where(tall == moved, 0.5, 0.0).astype(BF16)
            pick[i, :, NODES * k : NODES * (k + 1)] = hot
    wide_lanes = PARTS * NODES
    r0 = iota((wide_lanes, wide_lanes), 0)
    goal = ((r0 >> 5) & 3) * NODES + (r0 >> 7) * HALO + (r0 & 31)
    perm[...] = jnp.where(iota((wide_lanes, wide_lanes), 1) == goal, 1.0, 0.0).astype(BF16)

    def region(p, s):
        r = lax.rem(row + p + member_count, member_count)
        c = lax.rem(column + s + space_count, space_count)
        return r * space_count + c

    def weight(names, p, s, base):
        held = jnp.sum(
            jnp.where(names == region(p, base + s), 1.0, 0.0), axis=1, keepdims=True
        )
        return held * (1.0 / (1.0 + (p * p + s * s) / 2.0))

    for copy in member_copies:
        copy.wait_recv()
    for i in range(2):
        list_copies[2 * i + 1].wait_recv()
    rows = [(-1, gram_member[0].astype(F32)), (0, gram_own[...]), (1, gram_member[1].astype(F32))]
    for i, (offset, s) in enumerate(((1, -1), (-1, 1))):
        names = nears[1 - i]
        total = sum(weight(names, p, s, offset) * values for p, values in rows)
        sum_send[i, 0:ENSEMBLE, :] = total[0:ENSEMBLE].astype(BF16)
        sum_send[i, ENSEMBLE:, :] = forcing_rows(
            jnp.sum(total[ENSEMBLE:], axis=0, keepdims=True)
        ).astype(BF16)
    sum_copies = [
        remote(
            sum_send.at[i], sum_recv.at[i], sum_send_sem.at[i], sum_recv_sem.at[i], at_space(offset)
        )
        for i, offset in enumerate((1, -1))
    ]
    for copy in sum_copies:
        copy.start()

    for copy in halo_copies:
        copy.wait_recv()

    both = jnp.concatenate([halo_recv[0], halo_recv[1]], axis=1)
    ordered = dot(both, perm_halo[...]).astype(BF16)
    for g in range(0, groups, HALO_STEP):
        wide = jnp.concatenate(
            [ordered[CHANNELS * t : CHANNELS * (t + 1)] for t in range(g, g + HALO_STEP)], axis=1
        )
        rounded = dot(we_t[...], wide).astype(BF16)
        values = dot(wsr_t[0:HIDDEN, :], rounded).astype(BF16)
        for t in range(2 * HALO_STEP):
            sh[2 * g + t] = values[:, NODES * t : NODES * (t + 1)]

    strip = 64
    members = MEMBERS // MEMBER_CHUNKS
    x_copies = []

    def gather(g):
        for i in range(2):
            left = jnp.concatenate(
                [
                    jnp.concatenate([se[PARTS * g + 2 * j + i], sh[2 * g + j]], axis=1)
                    for j in range(2)
                ],
                axis=0,
            )
            vs[g % 2, i] = dot(left, pick[i])

    def message(g):
        for i in range(2):
            for j in range(2):
                q = 2 * j + i
                square = jnp.zeros((8, NODES), F32)
                for top in range(0, HIDDEN, strip):
                    base = rv[PARTS * g + q, top : top + strip, :]
                    total = None
                    for k in range(SLOTS):
                        half = (
                            vs[
                                g % 2,
                                i,
                                HIDDEN * j + top : HIDDEN * j + top + strip,
                                NODES * k : NODES * (k + 1),
                            ]
                            + base
                        )
                        term = half + half * jnp.tanh(half)
                        total = term if total is None else total + term
                    ms[q, top : top + strip, :] = total
                    squared = total * total
                    for t in range(0, strip, 8):
                        square = square + squared[t : t + 8]
                mean_square = jnp.sum(square, axis=0, keepdims=True) * (1.0 / HIDDEN)
                scale = lax.rsqrt(mean_square + EPSILON)
                for top in range(0, HIDDEN, strip):
                    nb[g % 2, top : top + strip, NODES * q : NODES * (q + 1)] = (
                        ms[q, top : top + strip, :] * scale * gain_col[top : top + strip, :]
                    ).astype(BF16)

    def update(g):
        wide = jnp.concatenate([fv[PARTS * g + q] for q in range(PARTS)], axis=1)
        final = (dot(we_t[...], wide) + dot(wu_t[...], nb[g % 2])).astype(BF16)
        values = dot(wd_t[...], final) + wide.astype(F32)
        chunk, place = divmod(PARTS * g, members)
        for q in range(PARTS):
            top = (place + q) * CHANNELS
            fs[chunk % 2, top : top + CHANNELS, :] = values[:, NODES * q : NODES * (q + 1)]
        if place + PARTS < members:
            return
        packed = jnp.concatenate(
            [
                jnp.concatenate(
                    [
                        fs[chunk % 2, pl.ds(PARTS * cg + c, members, stride=CHANNELS), :]
                        for c in range(PARTS)
                    ],
                    axis=1,
                )
                for cg in range(CHANNELS // PARTS)
            ],
            axis=0,
        ).astype(BF16)
        turned = dot(packed, perm[...]).astype(BF16)
        for target in range(PARTS):
            sb[target, chunk] = turned[:, NODES * target : NODES * (target + 1)]
        for d in range(1, PARTS):
            device = at_member(d)
            copy = remote(
                sb.at[device[0], chunk],
                xr.at[row, chunk],
                x_send_sem.at[chunk, d - 1],
                x_recv_sem.at[chunk, d - 1],
                device,
            )
            copy.start()
            x_copies.append(copy)
        xr[row, chunk] = sb[row, chunk]

    for g in range(groups + 2):
        if g < groups:
            gather(g)
        if 1 <= g <= groups:
            message(g - 1)
        if g >= 2:
            update(g - 2)

    for copy in sum_copies + far_copies:
        copy.wait_recv()
    names = near_ref[...]
    total = gram_own[...] + sum_recv[0].astype(F32) + sum_recv[1].astype(F32)
    for values, p, s in (
        (gram_member[0], -1, 0),
        (gram_member[1], 1, 0),
        (gram_far[0], 0, -2),
        (gram_far[1], 0, 2),
    ):
        total = total + weight(names, p, s, 0) * values.astype(F32)
    forcing = jnp.sum(total[ENSEMBLE:], axis=0, keepdims=True)
    identity = eye(ENSEMBLE, F32)
    system = identity + total[0:ENSEMBLE] / (ENSEMBLE - 1)
    norm = jnp.sum(jnp.sum(system * system, axis=1, keepdims=True), axis=0, keepdims=True)
    scaling = jnp.sqrt(norm)
    iterate = system / scaling
    inverse = identity

    def full(left, right):
        return jnp.dot(left, right, precision=FULL_PRECISION, preferred_element_type=F32)

    for _ in range(ITERS_NS):
        correction = 1.5 * identity - 0.5 * full(inverse, iterate)
        iterate = full(iterate, correction)
        inverse = full(correction, inverse)
    forcing = jnp.broadcast_to(forcing, (8, ENSEMBLE))
    mean_weights = full(full(forcing, inverse), inverse)[0:1] / (scaling * (ENSEMBLE - 1))
    root = inverse / jnp.sqrt(scaling)
    rest = (
        1.0
        - jnp.sum(root, axis=1, keepdims=True)
        - jnp.sum(mean_weights, axis=1, keepdims=True)
    ) * (1.0 / ENSEMBLE)
    lane = iota((ENSEMBLE, 2 * ENSEMBLE), 1)
    source = iota((ENSEMBLE, 2 * ENSEMBLE), 0)
    same = ((lane >> 4) == (source >> 3)) & ((lane & 7) == (source & 7))
    spread = [
        jnp.where(same & (((lane >> 3) & 1) == half), 1.0, 0.0).astype(BF16) for half in range(2)
    ]
    mix_high, mix_low = [
        jnp.concatenate([dot(part, s) for s in spread], axis=0).astype(BF16)
        for part in split(root + mean_weights + rest)
    ]

    for copy in x_copies:
        copy.wait_recv()
    per_chunk = CHANNELS // PARTS // CHANNEL_CHUNKS
    owned = MEMBERS
    z_copies = []
    for ch in range(CHANNEL_CHUNKS):
        states = jnp.concatenate(
            [
                jnp.concatenate(
                    [
                        xr[source, chunk, 16 * pair : 16 * (pair + 1), :]
                        for source in range(PARTS)
                        for chunk in range(MEMBER_CHUNKS)
                    ],
                    axis=0,
                )
                for pair in range(ch * per_chunk // 2, (ch + 1) * per_chunk // 2)
            ],
            axis=1,
        )
        mixed = (dot(mix_high, states) + dot(mix_low, states)).astype(BF16)
        for target in range(PARTS):
            for cg in range(per_chunk):
                top = ENSEMBLE * (cg % 2) + owned * target
                zs[target, ch, owned * cg : owned * (cg + 1), :] = mixed[
                    top : top + owned, NODES * (cg // 2) : NODES * (cg // 2 + 1)
                ]
        sent = []
        for d in range(1, PARTS):
            device = at_member(d)
            copy = remote(
                zs.at[device[0], ch],
                zr.at[row, ch],
                z_send_sem.at[ch, d - 1],
                z_recv_sem.at[ch, d - 1],
                device,
            )
            copy.start()
            sent.append(copy)
        z_copies.append(sent)
        zr[row, ch] = zs[row, ch]

    span = PARTS * per_chunk
    for ch in range(CHANNEL_CHUNKS):
        for copy in z_copies[ch]:
            copy.wait_recv()
        packed = jnp.concatenate([zr[source, ch] for source in range(PARTS)], axis=1)
        turned = dot(packed, perm[...])
        for cg in range(per_chunk):
            for c in range(PARTS):
                os_[pl.ds(PARTS * cg + c, owned, stride=span), :] = turned[
                    owned * cg : owned * (cg + 1), NODES * c : NODES * (c + 1)
                ]
        for j in range(owned):
            out_ref[j, span * ch : span * (ch + 1), :] = os_[span * j : span * (j + 1), :].astype(
                BF16
            )

    for copy in list_copies + member_copies + far_copies + halo_copies + sum_copies + x_copies:
        copy.wait_send()
    for sent in z_copies:
        for copy in sent:
            copy.wait_send()


def body(*arrays):
    arrays = list(arrays)
    for i in (6, 7):
        arrays[i] = arrays[i].T
    vmem = pl.BlockSpec(memory_space=pltpu.VMEM)
    dma = pltpu.SemaphoreType.DMA
    return pl.pallas_call(
        functools.partial(kernel, lax.axis_size("member"), lax.axis_size("space")),
        out_shape=jax.ShapeDtypeStruct((MEMBERS, CHANNELS, NODES), BF16),
        in_specs=[pl.BlockSpec(memory_space=pl.ANY)] * 12,
        out_specs=vmem,
        scratch_shapes=[
            pltpu.VMEM((MEMBERS, CHANNELS, NODES), BF16),
            pltpu.VMEM((CHANNELS, HIDDEN), BF16),
            pltpu.VMEM((1, HIDDEN, HIDDEN), BF16),
            pltpu.VMEM((1, HIDDEN, HIDDEN), BF16),
            pltpu.VMEM((1, HIDDEN, HIDDEN), BF16),
            pltpu.VMEM((1, HIDDEN), BF16),
            pltpu.VMEM((CHANNELS, HIDDEN), BF16),
            pltpu.VMEM((SLOTS, NODES), jnp.int32),
            pltpu.VMEM((2, HALO), jnp.int32),
            pltpu.VMEM((1, ENSEMBLE, HIDDEN), BF16),
            pltpu.VMEM((1, 2, HIDDEN), BF16),
            pltpu.VMEM((1, 8), jnp.int32),
            pltpu.VMEM((HIDDEN, CHANNELS), BF16),
            pltpu.VMEM((2 * HIDDEN, HIDDEN), BF16),
            pltpu.VMEM((HIDDEN, HIDDEN), BF16),
            pltpu.VMEM((HIDDEN, NODES), F32),
            pltpu.VMEM((2, HIDDEN, SLOTS * NODES), BF16),
            pltpu.VMEM((PARTS * NODES, PARTS * NODES), BF16),
            pltpu.VMEM((HIDDEN, HIDDEN), BF16),
            pltpu.VMEM((2, 2, HALO), jnp.int32),
            pltpu.VMEM((2, 1, 8), jnp.int32),
            pltpu.VMEM((2, MEMBERS // PARTS * CHANNELS, NODES), BF16),
            pltpu.VMEM((2, MEMBERS // PARTS * CHANNELS, NODES), BF16),
            pltpu.VMEM((MEMBERS, HIDDEN, NODES), BF16),
            pltpu.VMEM((MEMBERS, HIDDEN, NODES), F32),
            pltpu.VMEM((MEMBERS // 2, HIDDEN, NODES), BF16),
            pltpu.VMEM((2, 2, 2 * HIDDEN, SLOTS * NODES), F32),
            pltpu.VMEM((PARTS, HIDDEN, NODES), F32),
            pltpu.VMEM((2, HIDDEN, PARTS * NODES), BF16),
            pltpu.VMEM((2, MEMBERS // MEMBER_CHUNKS * CHANNELS, NODES), F32),
            pltpu.VMEM((PARTS, MEMBER_CHUNKS, 512 // MEMBER_CHUNKS, NODES), BF16),
            pltpu.VMEM((PARTS, MEMBER_CHUNKS, 512 // MEMBER_CHUNKS, NODES), BF16),
            pltpu.VMEM((PARTS, CHANNEL_CHUNKS, 512 // CHANNEL_CHUNKS, NODES), BF16),
            pltpu.VMEM((PARTS, CHANNEL_CHUNKS, 512 // CHANNEL_CHUNKS, NODES), BF16),
            pltpu.VMEM((MEMBERS * CHANNELS // CHANNEL_CHUNKS, NODES), F32),
            pltpu.VMEM((GRAM_ROWS, ENSEMBLE), F32),
            pltpu.VMEM((GRAM_ROWS, ENSEMBLE), BF16),
            pltpu.VMEM((2, GRAM_ROWS, ENSEMBLE), BF16),
            pltpu.VMEM((2, GRAM_ROWS, ENSEMBLE), BF16),
            pltpu.VMEM((2, GRAM_ROWS, ENSEMBLE), BF16),
            pltpu.VMEM((2, GRAM_ROWS, ENSEMBLE), BF16),
            dma((12,)),
            dma((2,)),
            dma((2,)),
            dma((2,)),
            dma((2,)),
            dma((2,)),
            dma((2,)),
            dma((2,)),
            dma((2,)),
            dma((2,)),
            dma((2,)),
            dma((2,)),
            dma((2,)),
            dma((MEMBER_CHUNKS, PARTS - 1)),
            dma((MEMBER_CHUNKS, PARTS - 1)),
            dma((CHANNEL_CHUNKS, PARTS - 1)),
            dma((CHANNEL_CHUNKS, PARTS - 1)),
        ],
        compiler_params=pltpu.CompilerParams(collective_id=0, has_side_effects=True),
        name="cycle",
    )(*arrays)


def solution(mesh):
    placed = (
        P("member", None, "space"),
        P(),
        P(),
        P(),
        P(),
        P(),
        P(),
        P("space", None),
        P(None, "space"),
        P(("member", "space"), None, None),
        P(("member", "space"), None, None),
        P(("member", "space"), None),
    )
    return jax.shard_map(
        body, mesh=mesh, in_specs=placed, out_specs=P("member", None, "space"), check_vma=False
    )
```

```python
import functools

import jax
import jax.numpy as jnp
from jax import lax
from jax.experimental import pallas as pl
from jax.experimental.pallas import tpu as pltpu
from jax.sharding import PartitionSpec as P

ITERS_NS = 5
EPSILON = 1e-05
FULL_PRECISION = lax.Precision.HIGHEST
MESH = pl.DeviceIdType.MESH
BF16 = jnp.bfloat16
F32 = jnp.float32

MEMBERS = 32
CHANNELS = 64
NODES = 128
HIDDEN = 256
HALO = 32
SLOTS = 4
PARTS = 4
ENSEMBLE = 128
GRAM_ROWS = 144
MEMBER_CHUNKS = 4
CHANNEL_CHUNKS = 4
OWN_STEP = 16


def dot(left, right):
    return jnp.dot(left, right, preferred_element_type=F32)


def dot_nt(left, right):
    return lax.dot_general(left, right, (((1,), (1,)), ((), ())), preferred_element_type=F32)


def iota(shape, dim):
    return lax.broadcasted_iota(jnp.int32, shape, dim)


def eye(extent, dtype):
    return jnp.where(iota((extent, extent), 0) == iota((extent, extent), 1), 1.0, 0.0).astype(dtype)


def split(values):
    high = values.astype(BF16)
    return high, (values - high.astype(F32)).astype(BF16)


def kernel(
    member_count,
    space_count,
    fields_hbm,
    we_hbm,
    ws_hbm,
    wr_hbm,
    wu_hbm,
    gain_hbm,
    wd_hbm,
    edge_hbm,
    halo_hbm,
    pert_hbm,
    vals_hbm,
    near_hbm,
    out_ref,
    fv,
    we_ref,
    ws_ref,
    wr_ref,
    wu_ref,
    gain_ref,
    wd_t,
    edge_ref,
    halo_ref,
    pert_ref,
    vals_ref,
    near_ref,
    we_t,
    wsr_t,
    wu_t,
    gain_col,
    pick,
    perm,
    chooser,
    nears,
    halo_recv,
    se,
    rv,
    sh,
    vs,
    ms,
    nb,
    fs,
    sb,
    xr,
    zs,
    zr,
    os_,
    gram_own,
    gram_send,
    gram_member,
    sum_send,
    sum_recv,
    gram_far,
    load_sem,
    near_send_sem,
    near_recv_sem,
    halo_send_sem,
    halo_recv_sem,
    gm_send_sem,
    gm_recv_sem,
    sum_send_sem,
    sum_recv_sem,
    far_send_sem,
    far_recv_sem,
    x_send_sem,
    x_recv_sem,
    z_send_sem,
    z_recv_sem,
):
    row = lax.axis_index("member")
    column = lax.axis_index("space")

    def at_member(offset):
        return (lax.rem(row + offset + member_count, member_count), column)

    def at_space(offset):
        return (row, lax.rem(column + offset + space_count, space_count))

    def remote(source, target, send_sem, recv_sem, device):
        return pltpu.make_async_remote_copy(
            src_ref=source,
            dst_ref=target,
            send_sem=send_sem,
            recv_sem=recv_sem,
            device_id=device,
            device_id_type=MESH,
        )

    barrier = pltpu.get_barrier_semaphore()
    partners = [at_space(-1), at_space(1), at_space(-2), at_space(2)]
    partners += [at_member(d) for d in range(1, PARTS)]
    for partner in partners:
        pl.semaphore_signal(barrier, inc=1, device_id=partner, device_id_type=MESH)

    sources = (halo_hbm, near_hbm, pert_hbm, vals_hbm, we_hbm, ws_hbm, wr_hbm, fields_hbm)
    sources += (edge_hbm, wu_hbm, gain_hbm, wd_hbm)
    targets = (halo_ref, near_ref, pert_ref, vals_ref, we_ref, ws_ref, wr_ref, fv)
    targets += (edge_ref, wu_ref, gain_ref, wd_t)
    loads = [
        pltpu.make_async_copy(source, target, load_sem.at[i])
        for i, (source, target) in enumerate(zip(sources, targets))
    ]
    for load in loads:
        load.start()

    eye_hidden = eye(HIDDEN, BF16)
    for load in loads[0:4]:
        load.wait()
    repeat = jnp.where(
        iota((HALO, HIDDEN), 0) == (iota((HALO, HIDDEN), 1) & (HALO - 1)), 1.0, 0.0
    ).astype(BF16)
    lane = iota((NODES, HIDDEN), 1)
    after = ((lane >> 5) & 1) == 1
    names = [
        jnp.broadcast_to(
            dot(
                jnp.broadcast_to(halo_ref[i : i + 1, :].astype(F32), (8, HALO)).astype(BF16), repeat
            )[0:1],
            (NODES, HIDDEN),
        )
        for i in range(2)
    ]
    names = jnp.where(after, names[1], names[0]).astype(jnp.int32)
    hit = names == iota((NODES, HIDDEN), 0)
    for i in range(2):
        for q in range(PARTS):
            chosen = hit & (after == (i == 1)) & ((lane >> 6) == q)
            top = NODES * (PARTS * i + q)
            chooser[top : top + NODES, :] = jnp.where(chosen, 1.0, 0.0).astype(BF16)

    pert = pert_ref[0]
    variance = vals_ref[0, 0:1, :].astype(F32)
    innovation = vals_ref[0, 1:2, :].astype(F32)
    scaled_high, scaled_low = split(pert.astype(F32) * variance)
    gram = dot_nt(scaled_high, pert) + dot_nt(scaled_low, pert)
    force_high, force_low = split(variance * innovation)
    sub = iota((16, HIDDEN), 0)
    force_rows = jnp.where(
        sub == 0,
        jnp.broadcast_to(force_high.astype(F32), (16, HIDDEN)),
        jnp.where(sub == 1, jnp.broadcast_to(force_low.astype(F32), (16, HIDDEN)), 0.0),
    ).astype(BF16)
    forcing = jnp.sum(dot_nt(force_rows, pert), axis=0, keepdims=True)
    sub16 = iota((16, ENSEMBLE), 0)

    def forcing_rows(values):
        high = values.astype(BF16).astype(F32)
        low = values - high
        return jnp.where(
            sub16 == 0,
            jnp.broadcast_to(high, (16, ENSEMBLE)),
            jnp.where(sub16 == 1, jnp.broadcast_to(low, (16, ENSEMBLE)), 0.0),
        )

    gram_own[0:ENSEMBLE, :] = gram
    gram_own[ENSEMBLE:GRAM_ROWS, :] = forcing_rows(forcing)
    gram_send[...] = gram_own[...].astype(BF16)

    for load in loads[4:]:
        load.wait()
    pl.semaphore_wait(barrier, len(partners))

    near_copies = [
        remote(near_ref, nears.at[i], near_send_sem.at[i], near_recv_sem.at[i], at_space(offset))
        for i, offset in enumerate((1, -1))
    ]
    for copy in near_copies:
        copy.start()
    members = MEMBERS // MEMBER_CHUNKS
    halo_copies = []
    for chunk in range(MEMBER_CHUNKS):
        part = pl.ds(members * chunk, members)
        for i, offset in enumerate((1, -1)):
            copy = remote(
                fv.at[part],
                halo_recv.at[i, part],
                halo_send_sem.at[chunk, i],
                halo_recv_sem.at[chunk, i],
                at_space(offset),
            )
            copy.start()
            halo_copies.append(copy)
    member_copies = [
        remote(gram_send, gram_member.at[i], gm_send_sem.at[i], gm_recv_sem.at[i], at_member(offset))
        for i, offset in enumerate((1, -1))
    ]
    far_copies = [
        remote(gram_send, gram_far.at[i], far_send_sem.at[i], far_recv_sem.at[i], at_space(offset))
        for i, offset in enumerate((2, -2))
    ]
    for copy in member_copies + far_copies:
        copy.start()

    we_t[...] = dot_nt(eye_hidden, we_ref[...]).astype(BF16)
    wsr_t[0:HIDDEN, :] = dot_nt(eye_hidden, ws_ref[0]).astype(BF16)
    wsr_t[HIDDEN:, :] = (dot_nt(eye_hidden, wr_ref[0]) * 0.5).astype(BF16)

    groups = MEMBERS // PARTS
    for m in range(0, MEMBERS, OWN_STEP):
        wide = jnp.concatenate([fv[m + t] for t in range(OWN_STEP)], axis=1)
        rounded = dot(we_t[...], wide).astype(BF16)
        both = dot(wsr_t[...], rounded)
        for t in range(OWN_STEP):
            se[m + t] = both[0:HIDDEN, NODES * t : NODES * (t + 1)].astype(BF16)
            rv[m + t] = both[HIDDEN:, NODES * t : NODES * (t + 1)]

    wu_t[...] = dot_nt(eye_hidden, wu_ref[0]).astype(BF16)
    gain_col[...] = dot_nt(eye_hidden, jnp.broadcast_to(gain_ref[...], (NODES, HIDDEN)))
    tall = iota((HIDDEN, NODES), 0)
    for k in range(SLOTS):
        sender = jnp.broadcast_to(edge_ref[k : k + 1, :], (HIDDEN, NODES))
        for i in range(2):
            moved = sender + jnp.where(sender >= NODES, 2 * HALO * i, 0)
            hot = jnp.where(tall == moved, 0.5, 0.0).astype(BF16)
            pick[i, :, NODES * k : NODES * (k + 1)] = hot
    wide_lanes = PARTS * NODES
    r0 = iota((wide_lanes, wide_lanes), 0)
    goal = ((r0 >> 5) & 3) * NODES + (r0 >> 7) * HALO + (r0 & 31)
    perm[...] = jnp.where(iota((wide_lanes, wide_lanes), 1) == goal, 1.0, 0.0).astype(BF16)

    def halo(chunk):
        for copy in halo_copies[2 * chunk : 2 * chunk + 2]:
            copy.wait_recv()
        first = members * chunk
        both = jnp.concatenate(
            [
                jnp.concatenate(
                    [
                        halo_recv[i, first + PARTS * t + q]
                        for i in range(2)
                        for q in range(PARTS)
                    ],
                    axis=1,
                )
                for t in range(members // PARTS)
            ],
            axis=0,
        )
        ordered = dot(both, chooser[...]).astype(BF16)
        wide = jnp.concatenate(
            [ordered[CHANNELS * t : CHANNELS * (t + 1)] for t in range(members // PARTS)], axis=1
        )
        rounded = dot(we_t[...], wide).astype(BF16)
        values = dot(wsr_t[0:HIDDEN, :], rounded).astype(BF16)
        for t in range(members // 2):
            sh[first // 2 + t] = values[:, NODES * t : NODES * (t + 1)]

    def region(p, s):
        r = lax.rem(row + p + member_count, member_count)
        c = lax.rem(column + s + space_count, space_count)
        return r * space_count + c

    def weight(names, p, s, base):
        held = jnp.sum(
            jnp.where(names == region(p, base + s), 1.0, 0.0), axis=1, keepdims=True
        )
        return held * (1.0 / (1.0 + (p * p + s * s) / 2.0))

    sum_copies = []

    def send_sums():
        for copy in member_copies:
            copy.wait_recv()
        for copy in near_copies:
            copy.wait_recv()
        rows = [(-1, gram_member[0].astype(F32)), (0, gram_own[...]), (1, gram_member[1].astype(F32))]
        for i, (offset, s) in enumerate(((1, -1), (-1, 1))):
            names = nears[1 - i]
            total = sum(weight(names, p, s, offset) * values for p, values in rows)
            sum_send[i, 0:ENSEMBLE, :] = total[0:ENSEMBLE].astype(BF16)
            sum_send[i, ENSEMBLE:, :] = forcing_rows(
                jnp.sum(total[ENSEMBLE:], axis=0, keepdims=True)
            ).astype(BF16)
        for i, offset in enumerate((1, -1)):
            copy = remote(
                sum_send.at[i], sum_recv.at[i], sum_send_sem.at[i], sum_recv_sem.at[i], at_space(offset)
            )
            copy.start()
            sum_copies.append(copy)
    strip = 64
    x_copies = []

    def gather(g):
        for i in range(2):
            left = jnp.concatenate(
                [
                    jnp.concatenate([se[PARTS * g + 2 * j + i], sh[2 * g + j]], axis=1)
                    for j in range(2)
                ],
                axis=0,
            )
            vs[g % 2, i] = dot(left, pick[i])

    def message(g):
        for i in range(2):
            for j in range(2):
                q = 2 * j + i
                square = jnp.zeros((8, NODES), F32)
                for top in range(0, HIDDEN, strip):
                    base = rv[PARTS * g + q, top : top + strip, :]
                    total = None
                    for k in range(SLOTS):
                        half = (
                            vs[
                                g % 2,
                                i,
                                HIDDEN * j + top : HIDDEN * j + top + strip,
                                NODES * k : NODES * (k + 1),
                            ]
                            + base
                        )
                        term = half + half * jnp.tanh(half)
                        total = term if total is None else total + term
                    ms[q, top : top + strip, :] = total
                    squared = total * total
                    for t in range(0, strip, 8):
                        square = square + squared[t : t + 8]
                mean_square = jnp.sum(square, axis=0, keepdims=True) * (1.0 / HIDDEN)
                scale = lax.rsqrt(mean_square + EPSILON)
                for top in range(0, HIDDEN, strip):
                    nb[g % 2, top : top + strip, NODES * q : NODES * (q + 1)] = (
                        ms[q, top : top + strip, :] * scale * gain_col[top : top + strip, :]
                    ).astype(BF16)

    def update(g):
        wide = jnp.concatenate([fv[PARTS * g + q] for q in range(PARTS)], axis=1)
        final = (dot(we_t[...], wide) + dot(wu_t[...], nb[g % 2])).astype(BF16)
        values = dot(wd_t[...], final) + wide.astype(F32)
        chunk, place = divmod(PARTS * g, members)
        for q in range(PARTS):
            top = (place + q) * CHANNELS
            fs[chunk % 2, top : top + CHANNELS, :] = values[:, NODES * q : NODES * (q + 1)]
        if place + PARTS < members:
            return
        packed = jnp.concatenate(
            [
                jnp.concatenate(
                    [
                        fs[chunk % 2, pl.ds(PARTS * cg + c, members, stride=CHANNELS), :]
                        for c in range(PARTS)
                    ],
                    axis=1,
                )
                for cg in range(CHANNELS // PARTS)
            ],
            axis=0,
        ).astype(BF16)
        turned = dot(packed, perm[...]).astype(BF16)
        for target in range(PARTS):
            sb[target, chunk] = turned[:, NODES * target : NODES * (target + 1)]
        for d in range(1, PARTS):
            device = at_member(d)
            copy = remote(
                sb.at[device[0], chunk],
                xr.at[row, chunk],
                x_send_sem.at[chunk, d - 1],
                x_recv_sem.at[chunk, d - 1],
                device,
            )
            copy.start()
            x_copies.append(copy)
        xr[row, chunk] = sb[row, chunk]

    for chunk in range(MEMBER_CHUNKS):
        halo(chunk)
        first = chunk * members // PARTS
        last = first + members // PARTS
        gather(first)
        for g in range(first, last):
            if g + 1 < last:
                gather(g + 1)
            message(g)
            if g > first:
                update(g - 1)
        update(last - 1)
        if chunk == 0:
            send_sums()

    for copy in sum_copies + far_copies:
        copy.wait_recv()
    names = near_ref[...]
    total = gram_own[...] + sum_recv[0].astype(F32) + sum_recv[1].astype(F32)
    for values, p, s in (
        (gram_member[0], -1, 0),
        (gram_member[1], 1, 0),
        (gram_far[0], 0, -2),
        (gram_far[1], 0, 2),
    ):
        total = total + weight(names, p, s, 0) * values.astype(F32)
    forcing = jnp.sum(total[ENSEMBLE:], axis=0, keepdims=True)
    identity = eye(ENSEMBLE, F32)
    system = identity + total[0:ENSEMBLE] / (ENSEMBLE - 1)
    norm = jnp.sum(jnp.sum(system * system, axis=1, keepdims=True), axis=0, keepdims=True)
    scaling = jnp.sqrt(norm)
    iterate = system / scaling
    inverse = identity

    def full(left, right):
        return jnp.dot(left, right, precision=FULL_PRECISION, preferred_element_type=F32)

    for _ in range(ITERS_NS):
        correction = 1.5 * identity - 0.5 * full(inverse, iterate)
        iterate = full(iterate, correction)
        inverse = full(correction, inverse)
    forcing = jnp.broadcast_to(forcing, (8, ENSEMBLE))
    mean_weights = full(full(forcing, inverse), inverse)[0:1] / (scaling * (ENSEMBLE - 1))
    root = inverse / jnp.sqrt(scaling)
    rest = (
        1.0
        - jnp.sum(root, axis=1, keepdims=True)
        - jnp.sum(mean_weights, axis=1, keepdims=True)
    ) * (1.0 / ENSEMBLE)
    lane = iota((ENSEMBLE, 2 * ENSEMBLE), 1)
    source = iota((ENSEMBLE, 2 * ENSEMBLE), 0)
    same = ((lane >> 4) == (source >> 3)) & ((lane & 7) == (source & 7))
    spread = [
        jnp.where(same & (((lane >> 3) & 1) == half), 1.0, 0.0).astype(BF16) for half in range(2)
    ]
    mix_high, mix_low = [
        jnp.concatenate([dot(part, s) for s in spread], axis=0).astype(BF16)
        for part in split(root + mean_weights + rest)
    ]

    for copy in x_copies:
        copy.wait_recv()
    per_chunk = CHANNELS // PARTS // CHANNEL_CHUNKS
    owned = MEMBERS
    z_copies = []
    for ch in range(CHANNEL_CHUNKS):
        states = jnp.concatenate(
            [
                jnp.concatenate(
                    [
                        xr[source, chunk, 16 * pair : 16 * (pair + 1), :]
                        for source in range(PARTS)
                        for chunk in range(MEMBER_CHUNKS)
                    ],
                    axis=0,
                )
                for pair in range(ch * per_chunk // 2, (ch + 1) * per_chunk // 2)
            ],
            axis=1,
        )
        mixed = (dot(mix_high, states) + dot(mix_low, states)).astype(BF16)
        for target in range(PARTS):
            for cg in range(per_chunk):
                top = ENSEMBLE * (cg % 2) + owned * target
                zs[target, ch, owned * cg : owned * (cg + 1), :] = mixed[
                    top : top + owned, NODES * (cg // 2) : NODES * (cg // 2 + 1)
                ]
        sent = []
        for d in range(1, PARTS):
            device = at_member(d)
            copy = remote(
                zs.at[device[0], ch],
                zr.at[row, ch],
                z_send_sem.at[ch, d - 1],
                z_recv_sem.at[ch, d - 1],
                device,
            )
            copy.start()
            sent.append(copy)
        z_copies.append(sent)
        zr[row, ch] = zs[row, ch]

    span = PARTS * per_chunk
    for ch in range(CHANNEL_CHUNKS):
        for copy in z_copies[ch]:
            copy.wait_recv()
        packed = jnp.concatenate([zr[source, ch] for source in range(PARTS)], axis=1)
        turned = dot(packed, perm[...])
        for cg in range(per_chunk):
            for c in range(PARTS):
                os_[pl.ds(PARTS * cg + c, owned, stride=span), :] = turned[
                    owned * cg : owned * (cg + 1), NODES * c : NODES * (c + 1)
                ]
        for j in range(owned):
            out_ref[j, span * ch : span * (ch + 1), :] = os_[span * j : span * (j + 1), :].astype(
                BF16
            )

    for copy in near_copies + member_copies + far_copies + halo_copies + sum_copies + x_copies:
        copy.wait_send()
    for sent in z_copies:
        for copy in sent:
            copy.wait_send()


def body(*arrays):
    arrays = list(arrays)
    for i in (6, 7):
        arrays[i] = arrays[i].T
    vmem = pl.BlockSpec(memory_space=pltpu.VMEM)
    dma = pltpu.SemaphoreType.DMA
    return pl.pallas_call(
        functools.partial(kernel, lax.axis_size("member"), lax.axis_size("space")),
        out_shape=jax.ShapeDtypeStruct((MEMBERS, CHANNELS, NODES), BF16),
        in_specs=[pl.BlockSpec(memory_space=pl.ANY)] * 12,
        out_specs=vmem,
        scratch_shapes=[
            pltpu.VMEM((MEMBERS, CHANNELS, NODES), BF16),
            pltpu.VMEM((CHANNELS, HIDDEN), BF16),
            pltpu.VMEM((1, HIDDEN, HIDDEN), BF16),
            pltpu.VMEM((1, HIDDEN, HIDDEN), BF16),
            pltpu.VMEM((1, HIDDEN, HIDDEN), BF16),
            pltpu.VMEM((1, HIDDEN), BF16),
            pltpu.VMEM((CHANNELS, HIDDEN), BF16),
            pltpu.VMEM((SLOTS, NODES), jnp.int32),
            pltpu.VMEM((2, HALO), jnp.int32),
            pltpu.VMEM((1, ENSEMBLE, HIDDEN), BF16),
            pltpu.VMEM((1, 2, HIDDEN), BF16),
            pltpu.VMEM((1, 8), jnp.int32),
            pltpu.VMEM((HIDDEN, CHANNELS), BF16),
            pltpu.VMEM((2 * HIDDEN, HIDDEN), BF16),
            pltpu.VMEM((HIDDEN, HIDDEN), BF16),
            pltpu.VMEM((HIDDEN, NODES), F32),
            pltpu.VMEM((2, HIDDEN, SLOTS * NODES), BF16),
            pltpu.VMEM((PARTS * NODES, PARTS * NODES), BF16),
            pltpu.VMEM((2 * PARTS * NODES, HIDDEN), BF16),
            pltpu.VMEM((2, 1, 8), jnp.int32),
            pltpu.VMEM((2, MEMBERS, CHANNELS, NODES), BF16),
            pltpu.VMEM((MEMBERS, HIDDEN, NODES), BF16),
            pltpu.VMEM((MEMBERS, HIDDEN, NODES), F32),
            pltpu.VMEM((MEMBERS // 2, HIDDEN, NODES), BF16),
            pltpu.VMEM((2, 2, 2 * HIDDEN, SLOTS * NODES), F32),
            pltpu.VMEM((PARTS, HIDDEN, NODES), F32),
            pltpu.VMEM((2, HIDDEN, PARTS * NODES), BF16),
            pltpu.VMEM((2, MEMBERS // MEMBER_CHUNKS * CHANNELS, NODES), F32),
            pltpu.VMEM((PARTS, MEMBER_CHUNKS, 512 // MEMBER_CHUNKS, NODES), BF16),
            pltpu.VMEM((PARTS, MEMBER_CHUNKS, 512 // MEMBER_CHUNKS, NODES), BF16),
            pltpu.VMEM((PARTS, CHANNEL_CHUNKS, 512 // CHANNEL_CHUNKS, NODES), BF16),
            pltpu.VMEM((PARTS, CHANNEL_CHUNKS, 512 // CHANNEL_CHUNKS, NODES), BF16),
            pltpu.VMEM((MEMBERS * CHANNELS // CHANNEL_CHUNKS, NODES), F32),
            pltpu.VMEM((GRAM_ROWS, ENSEMBLE), F32),
            pltpu.VMEM((GRAM_ROWS, ENSEMBLE), BF16),
            pltpu.VMEM((2, GRAM_ROWS, ENSEMBLE), BF16),
            pltpu.VMEM((2, GRAM_ROWS, ENSEMBLE), BF16),
            pltpu.VMEM((2, GRAM_ROWS, ENSEMBLE), BF16),
            pltpu.VMEM((2, GRAM_ROWS, ENSEMBLE), BF16),
            dma((12,)),
            dma((2,)),
            dma((2,)),
            dma((MEMBER_CHUNKS, 2)),
            dma((MEMBER_CHUNKS, 2)),
            dma((2,)),
            dma((2,)),
            dma((2,)),
            dma((2,)),
            dma((2,)),
            dma((2,)),
            dma((MEMBER_CHUNKS, PARTS - 1)),
            dma((MEMBER_CHUNKS, PARTS - 1)),
            dma((CHANNEL_CHUNKS, PARTS - 1)),
            dma((CHANNEL_CHUNKS, PARTS - 1)),
        ],
        compiler_params=pltpu.CompilerParams(collective_id=0, has_side_effects=True),
        name="cycle",
    )(*arrays)


def solution(mesh):
    placed = (
        P("member", None, "space"),
        P(),
        P(),
        P(),
        P(),
        P(),
        P(),
        P("space", None),
        P(None, "space"),
        P(("member", "space"), None, None),
        P(("member", "space"), None, None),
        P(("member", "space"), None),
    )
    return jax.shard_map(
        body, mesh=mesh, in_specs=placed, out_specs=P("member", None, "space"), check_vma=False
    )
```

```python
import functools

import jax
import jax.numpy as jnp
from jax import lax
from jax.experimental import pallas as pl
from jax.experimental.pallas import tpu as pltpu
from jax.sharding import PartitionSpec as P

ITERS_NS = 5
EPSILON = 1e-05
FULL_PRECISION = lax.Precision.HIGHEST
MESH = pl.DeviceIdType.MESH
BF16 = jnp.bfloat16
F32 = jnp.float32

MEMBERS = 32
CHANNELS = 64
NODES = 128
HIDDEN = 256
HALO = 32
SLOTS = 4
PARTS = 4
ENSEMBLE = 128
GRAM_ROWS = 144
MEMBER_CHUNKS = 4
CHANNEL_CHUNKS = 4
OWN_STEP = 16


def dot(left, right):
    return jnp.dot(left, right, preferred_element_type=F32)


def dot_nt(left, right):
    return lax.dot_general(left, right, (((1,), (1,)), ((), ())), preferred_element_type=F32)


def iota(shape, dim):
    return lax.broadcasted_iota(jnp.int32, shape, dim)


def eye(extent, dtype):
    return jnp.where(iota((extent, extent), 0) == iota((extent, extent), 1), 1.0, 0.0).astype(dtype)


def split(values):
    high = values.astype(BF16)
    return high, (values - high.astype(F32)).astype(BF16)


def kernel(
    member_count,
    space_count,
    fields_hbm,
    we_hbm,
    ws_hbm,
    wr_hbm,
    wu_hbm,
    gain_hbm,
    wd_hbm,
    edge_hbm,
    halo_hbm,
    pert_hbm,
    vals_hbm,
    near_hbm,
    out_ref,
    fv,
    we_ref,
    ws_ref,
    wr_ref,
    wu_ref,
    gain_ref,
    wd_t,
    edge_ref,
    halo_ref,
    pert_ref,
    vals_ref,
    near_ref,
    we_t,
    wsr_t,
    wu_t,
    gain_col,
    pick,
    perm,
    chooser,
    lists,
    nears,
    halo_recv,
    side_send,
    side_recv,
    se,
    rv,
    sh,
    vs,
    ms,
    nb,
    fs,
    sb,
    xr,
    zs,
    zr,
    os_,
    gram_own,
    gram_send,
    gram_member,
    sum_send,
    sum_recv,
    gram_side,
    load_sem,
    list_send_sem,
    list_recv_sem,
    near_send_sem,
    near_recv_sem,
    halo_send_sem,
    halo_recv_sem,
    side_send_sem,
    side_recv_sem,
    gm_send_sem,
    gm_recv_sem,
    sum_send_sem,
    sum_recv_sem,
    gs_send_sem,
    gs_recv_sem,
    x_send_sem,
    x_recv_sem,
    z_send_sem,
    z_recv_sem,
):
    row = lax.axis_index("member")
    column = lax.axis_index("space")

    def at_member(offset):
        return (lax.rem(row + offset + member_count, member_count), column)

    def at_space(offset):
        return (row, lax.rem(column + offset + space_count, space_count))

    def remote(source, target, send_sem, recv_sem, device):
        return pltpu.make_async_remote_copy(
            src_ref=source,
            dst_ref=target,
            send_sem=send_sem,
            recv_sem=recv_sem,
            device_id=device,
            device_id_type=MESH,
        )

    barrier = pltpu.get_barrier_semaphore()
    partners = [at_space(-1)] + [at_member(d) for d in range(1, PARTS)]
    for partner in partners:
        pl.semaphore_signal(barrier, inc=1, device_id=partner, device_id_type=MESH)

    sources = (halo_hbm, near_hbm, pert_hbm, vals_hbm, we_hbm, ws_hbm, wr_hbm, fields_hbm)
    sources += (edge_hbm, wu_hbm, gain_hbm, wd_hbm)
    targets = (halo_ref, near_ref, pert_ref, vals_ref, we_ref, ws_ref, wr_ref, fv)
    targets += (edge_ref, wu_ref, gain_ref, wd_t)
    loads = [
        pltpu.make_async_copy(source, target, load_sem.at[i])
        for i, (source, target) in enumerate(zip(sources, targets))
    ]
    for load in loads:
        load.start()

    eye_hidden = eye(HIDDEN, BF16)
    for load in loads[0:4]:
        load.wait()
    repeat = jnp.where(
        iota((HALO, HIDDEN), 0) == (iota((HALO, HIDDEN), 1) & (HALO - 1)), 1.0, 0.0
    ).astype(BF16)
    lane = iota((NODES, HIDDEN), 1)
    after = ((lane >> 5) & 1) == 1


    def spread_names(values):
        values = jnp.broadcast_to(values.astype(F32), (8, HALO)).astype(BF16)
        return jnp.broadcast_to(dot(values, repeat)[0:1], (NODES, HIDDEN)).astype(jnp.int32)

    hit = spread_names(halo_ref[0:1, :]) == iota((NODES, HIDDEN), 0)
    for q in range(PARTS):
        chosen = hit & jnp.logical_not(after) & ((lane >> 6) == q)
        chooser[NODES * q : NODES * (q + 1), :] = jnp.where(chosen, 1.0, 0.0).astype(BF16)
    kept = iota((NODES, HIDDEN), 0)
    kept = (kept >> 5) * (2 * HALO) + HALO + (kept & (HALO - 1))
    chooser[PARTS * NODES :, :] = jnp.where(lane == kept, 1.0, 0.0).astype(BF16)

    pert = pert_ref[0]
    variance = vals_ref[0, 0:1, :].astype(F32)
    innovation = vals_ref[0, 1:2, :].astype(F32)
    scaled_high, scaled_low = split(pert.astype(F32) * variance)
    gram = dot_nt(scaled_high, pert) + dot_nt(scaled_low, pert)
    force_high, force_low = split(variance * innovation)
    sub = iota((16, HIDDEN), 0)
    force_rows = jnp.where(
        sub == 0,
        jnp.broadcast_to(force_high.astype(F32), (16, HIDDEN)),
        jnp.where(sub == 1, jnp.broadcast_to(force_low.astype(F32), (16, HIDDEN)), 0.0),
    ).astype(BF16)
    forcing = jnp.sum(dot_nt(force_rows, pert), axis=0, keepdims=True)
    sub16 = iota((16, ENSEMBLE), 0)

    def forcing_rows(values):
        high = values.astype(BF16).astype(F32)
        low = values - high
        return jnp.where(
            sub16 == 0,
            jnp.broadcast_to(high, (16, ENSEMBLE)),
            jnp.where(sub16 == 1, jnp.broadcast_to(low, (16, ENSEMBLE)), 0.0),
        )

    gram_own[0:ENSEMBLE, :] = gram
    gram_own[ENSEMBLE:GRAM_ROWS, :] = forcing_rows(forcing)
    gram_send[...] = gram_own[...].astype(BF16)

    for load in loads[4:]:
        load.wait()
    pl.semaphore_wait(barrier, len(partners))

    list_copy = remote(halo_ref, lists, list_send_sem, list_recv_sem, at_space(1))
    near_copies = [
        remote(near_ref, nears.at[i], near_send_sem.at[i], near_recv_sem.at[i], at_space(offset))
        for i, offset in enumerate((1, -1))
    ]
    side_copies = [
        remote(gram_send, gram_side.at[i], gs_send_sem.at[i], gs_recv_sem.at[i], at_space(offset))
        for i, offset in enumerate((1, -1))
    ]
    member_copies = [
        remote(gram_send, gram_member.at[i], gm_send_sem.at[i], gm_recv_sem.at[i], at_member(offset))
        for i, offset in enumerate((1, -1))
    ]
    list_copy.start()
    near_copies[0].start()
    members = MEMBERS // MEMBER_CHUNKS
    halo_copies = []
    for chunk in range(MEMBER_CHUNKS):
        part = pl.ds(members * chunk, members)
        copy = remote(
            fv.at[part],
            halo_recv.at[part],
            halo_send_sem.at[chunk],
            halo_recv_sem.at[chunk],
            at_space(1),
        )
        copy.start()
        halo_copies.append(copy)
        if chunk == 0:
            side_copies[0].start()
    for copy in member_copies:
        copy.start()

    we_t[...] = dot_nt(eye_hidden, we_ref[...]).astype(BF16)
    wsr_t[0:HIDDEN, :] = dot_nt(eye_hidden, ws_ref[0]).astype(BF16)
    wsr_t[HIDDEN:, :] = (dot_nt(eye_hidden, wr_ref[0]) * 0.5).astype(BF16)

    groups = MEMBERS // PARTS
    for m in range(0, MEMBERS, OWN_STEP):
        wide = jnp.concatenate([fv[m + t] for t in range(OWN_STEP)], axis=1)
        rounded = dot(we_t[...], wide).astype(BF16)
        both = dot(wsr_t[...], rounded)
        for t in range(OWN_STEP):
            se[m + t] = both[0:HIDDEN, NODES * t : NODES * (t + 1)].astype(BF16)
            rv[m + t] = both[HIDDEN:, NODES * t : NODES * (t + 1)]

    wu_t[...] = dot_nt(eye_hidden, wu_ref[0]).astype(BF16)
    gain_col[...] = dot_nt(eye_hidden, jnp.broadcast_to(gain_ref[...], (NODES, HIDDEN)))
    tall = iota((HIDDEN, NODES), 0)
    for k in range(SLOTS):
        sender = jnp.broadcast_to(edge_ref[k : k + 1, :], (HIDDEN, NODES))
        for i in range(2):
            moved = sender + jnp.where(sender >= NODES, 2 * HALO * i, 0)
            hot = jnp.where(tall == moved, 0.5, 0.0).astype(BF16)
            pick[i, :, NODES * k : NODES * (k + 1)] = hot
    wide_lanes = PARTS * NODES
    r0 = iota((wide_lanes, wide_lanes), 0)
    goal = ((r0 >> 5) & 3) * NODES + (r0 >> 7) * HALO + (r0 & 31)
    perm[...] = jnp.where(iota((wide_lanes, wide_lanes), 1) == goal, 1.0, 0.0).astype(BF16)

    list_copy.wait_recv()
    near_copies[0].wait_recv()
    near_copies[1].start()
    hit = spread_names(lists[1:2, :])[:, 0:NODES] == iota((NODES, NODES), 0)
    block = iota((NODES, NODES), 1) >> 5
    wanted = jnp.concatenate(
        [jnp.where(hit & (block == q), 1.0, 0.0).astype(BF16) for q in range(PARTS)], axis=0
    )
    quads = jnp.concatenate(
        [
            jnp.concatenate([fv[PARTS * g + q] for g in range(groups)], axis=0)
            for q in range(PARTS)
        ],
        axis=1,
    )
    side_send[...] = dot(quads, wanted).astype(BF16)
    side_rows = members // PARTS * CHANNELS
    select_copies = []
    for chunk in range(MEMBER_CHUNKS):
        part = pl.ds(side_rows * chunk, side_rows)
        copy = remote(
            side_send.at[part],
            side_recv.at[part],
            side_send_sem.at[chunk],
            side_recv_sem.at[chunk],
            at_space(-1),
        )
        copy.start()
        select_copies.append(copy)
    side_copies[1].start()

    def halo(chunk):
        halo_copies[chunk].wait_recv()
        select_copies[chunk].wait_recv()
        first = members * chunk
        both = jnp.concatenate(
            [
                jnp.concatenate(
                    [halo_recv[first + PARTS * t + q] for q in range(PARTS)]
                    + [side_recv[CHANNELS * (first // PARTS + t) : CHANNELS * (first // PARTS + t + 1), :]],
                    axis=1,
                )
                for t in range(members // PARTS)
            ],
            axis=0,
        )
        ordered = dot(both, chooser[...]).astype(BF16)
        wide = jnp.concatenate(
            [ordered[CHANNELS * t : CHANNELS * (t + 1)] for t in range(members // PARTS)], axis=1
        )
        rounded = dot(we_t[...], wide).astype(BF16)
        values = dot(wsr_t[0:HIDDEN, :], rounded).astype(BF16)
        for t in range(members // 2):
            sh[first // 2 + t] = values[:, NODES * t : NODES * (t + 1)]

    def region(p, s):
        r = lax.rem(row + p + member_count, member_count)
        c = lax.rem(column + s + space_count, space_count)
        return r * space_count + c

    def weight(names, p, s, base):
        held = jnp.sum(
            jnp.where(names == region(p, base + s), 1.0, 0.0), axis=1, keepdims=True
        )
        return held * (1.0 / (1.0 + (p * p + s * s) / 2.0))

    sum_copies = []

    def send_sum(i):
        offset, s = ((1, -1), (-1, 1))[i]
        if i == 0:
            near_copies[1].wait_recv()
        side_copies[i].wait_recv()
        names = nears[1 - i]
        rows = [
            (-1, gram_member[0].astype(F32)),
            (0, gram_own[...]),
            (1, gram_member[1].astype(F32)),
        ]
        total = sum(weight(names, p, s, offset) * values for p, values in rows)
        total = total + weight(names, 0, 2 * s, offset) * gram_side[i].astype(F32)
        sum_send[i, 0:ENSEMBLE, :] = total[0:ENSEMBLE].astype(BF16)
        sum_send[i, ENSEMBLE:, :] = forcing_rows(
            jnp.sum(total[ENSEMBLE:], axis=0, keepdims=True)
        ).astype(BF16)
        copy = remote(
            sum_send.at[i], sum_recv.at[i], sum_send_sem.at[i], sum_recv_sem.at[i], at_space(offset)
        )
        copy.start()
        sum_copies.append(copy)

    for copy in member_copies:
        copy.wait_recv()
    send_sum(0)

    strip = 64
    x_copies = []

    def gather(g):
        for i in range(2):
            left = jnp.concatenate(
                [
                    jnp.concatenate([se[PARTS * g + 2 * j + i], sh[2 * g + j]], axis=1)
                    for j in range(2)
                ],
                axis=0,
            )
            vs[g % 2, i] = dot(left, pick[i])

    def message(g):
        for i in range(2):
            for j in range(2):
                q = 2 * j + i
                square = jnp.zeros((8, NODES), F32)
                for top in range(0, HIDDEN, strip):
                    base = rv[PARTS * g + q, top : top + strip, :]
                    total = None
                    for k in range(SLOTS):
                        half = (
                            vs[
                                g % 2,
                                i,
                                HIDDEN * j + top : HIDDEN * j + top + strip,
                                NODES * k : NODES * (k + 1),
                            ]
                            + base
                        )
                        term = half + half * jnp.tanh(half)
                        total = term if total is None else total + term
                    ms[q, top : top + strip, :] = total
                    squared = total * total
                    for t in range(0, strip, 8):
                        square = square + squared[t : t + 8]
                mean_square = jnp.sum(square, axis=0, keepdims=True) * (1.0 / HIDDEN)
                scale = lax.rsqrt(mean_square + EPSILON)
                for top in range(0, HIDDEN, strip):
                    nb[g % 2, top : top + strip, NODES * q : NODES * (q + 1)] = (
                        ms[q, top : top + strip, :] * scale * gain_col[top : top + strip, :]
                    ).astype(BF16)

    def update(g):
        wide = jnp.concatenate([fv[PARTS * g + q] for q in range(PARTS)], axis=1)
        final = (dot(we_t[...], wide) + dot(wu_t[...], nb[g % 2])).astype(BF16)
        values = dot(wd_t[...], final) + wide.astype(F32)
        chunk, place = divmod(PARTS * g, members)
        for q in range(PARTS):
            top = (place + q) * CHANNELS
            fs[chunk % 2, top : top + CHANNELS, :] = values[:, NODES * q : NODES * (q + 1)]
        if place + PARTS < members:
            return
        packed = jnp.concatenate(
            [
                jnp.concatenate(
                    [
                        fs[chunk % 2, pl.ds(PARTS * cg + c, members, stride=CHANNELS), :]
                        for c in range(PARTS)
                    ],
                    axis=1,
                )
                for cg in range(CHANNELS // PARTS)
            ],
            axis=0,
        ).astype(BF16)
        turned = dot(packed, perm[...]).astype(BF16)
        for target in range(PARTS):
            sb[target, chunk] = turned[:, NODES * target : NODES * (target + 1)]
        for d in range(1, PARTS):
            device = at_member(d)
            copy = remote(
                sb.at[device[0], chunk],
                xr.at[row, chunk],
                x_send_sem.at[chunk, d - 1],
                x_recv_sem.at[chunk, d - 1],
                device,
            )
            copy.start()
            x_copies.append(copy)
        xr[row, chunk] = sb[row, chunk]

    for chunk in range(MEMBER_CHUNKS):
        halo(chunk)
        first = chunk * members // PARTS
        last = first + members // PARTS
        gather(first)
        for g in range(first, last):
            if g + 1 < last:
                gather(g + 1)
            message(g)
            if g > first:
                update(g - 1)
        update(last - 1)
        if chunk == 0:
            send_sum(1)

    for copy in sum_copies:
        copy.wait_recv()
    names = near_ref[...]
    total = gram_own[...] + sum_recv[0].astype(F32) + sum_recv[1].astype(F32)
    for values, p, s in (
        (gram_member[0], -1, 0),
        (gram_member[1], 1, 0),
    ):
        total = total + weight(names, p, s, 0) * values.astype(F32)
    forcing = jnp.sum(total[ENSEMBLE:], axis=0, keepdims=True)
    identity = eye(ENSEMBLE, F32)
    system = identity + total[0:ENSEMBLE] / (ENSEMBLE - 1)
    norm = jnp.sum(jnp.sum(system * system, axis=1, keepdims=True), axis=0, keepdims=True)
    scaling = jnp.sqrt(norm)
    iterate = system / scaling
    inverse = identity

    def full(left, right):
        return jnp.dot(left, right, precision=FULL_PRECISION, preferred_element_type=F32)

    for _ in range(ITERS_NS):
        correction = 1.5 * identity - 0.5 * full(inverse, iterate)
        iterate = full(iterate, correction)
        inverse = full(correction, inverse)
    forcing = jnp.broadcast_to(forcing, (8, ENSEMBLE))
    mean_weights = full(full(forcing, inverse), inverse)[0:1] / (scaling * (ENSEMBLE - 1))
    root = inverse / jnp.sqrt(scaling)
    rest = (
        1.0
        - jnp.sum(root, axis=1, keepdims=True)
        - jnp.sum(mean_weights, axis=1, keepdims=True)
    ) * (1.0 / ENSEMBLE)
    lane = iota((ENSEMBLE, 2 * ENSEMBLE), 1)
    source = iota((ENSEMBLE, 2 * ENSEMBLE), 0)
    same = ((lane >> 4) == (source >> 3)) & ((lane & 7) == (source & 7))
    spread = [
        jnp.where(same & (((lane >> 3) & 1) == half), 1.0, 0.0).astype(BF16) for half in range(2)
    ]
    mix_high, mix_low = [
        jnp.concatenate([dot(part, s) for s in spread], axis=0).astype(BF16)
        for part in split(root + mean_weights + rest)
    ]

    for copy in x_copies:
        copy.wait_recv()
    per_chunk = CHANNELS // PARTS // CHANNEL_CHUNKS
    owned = MEMBERS
    z_copies = []
    for ch in range(CHANNEL_CHUNKS):
        states = jnp.concatenate(
            [
                jnp.concatenate(
                    [
                        xr[source, chunk, 16 * pair : 16 * (pair + 1), :]
                        for source in range(PARTS)
                        for chunk in range(MEMBER_CHUNKS)
                    ],
                    axis=0,
                )
                for pair in range(ch * per_chunk // 2, (ch + 1) * per_chunk // 2)
            ],
            axis=1,
        )
        mixed = (dot(mix_high, states) + dot(mix_low, states)).astype(BF16)
        for target in range(PARTS):
            for cg in range(per_chunk):
                top = ENSEMBLE * (cg % 2) + owned * target
                zs[target, ch, owned * cg : owned * (cg + 1), :] = mixed[
                    top : top + owned, NODES * (cg // 2) : NODES * (cg // 2 + 1)
                ]
        sent = []
        for d in range(1, PARTS):
            device = at_member(d)
            copy = remote(
                zs.at[device[0], ch],
                zr.at[row, ch],
                z_send_sem.at[ch, d - 1],
                z_recv_sem.at[ch, d - 1],
                device,
            )
            copy.start()
            sent.append(copy)
        z_copies.append(sent)
        zr[row, ch] = zs[row, ch]

    span = PARTS * per_chunk
    for ch in range(CHANNEL_CHUNKS):
        for copy in z_copies[ch]:
            copy.wait_recv()
        packed = jnp.concatenate([zr[source, ch] for source in range(PARTS)], axis=1)
        turned = dot(packed, perm[...])
        for cg in range(per_chunk):
            for c in range(PARTS):
                os_[pl.ds(PARTS * cg + c, owned, stride=span), :] = turned[
                    owned * cg : owned * (cg + 1), NODES * c : NODES * (c + 1)
                ]
        for j in range(owned):
            out_ref[j, span * ch : span * (ch + 1), :] = os_[span * j : span * (j + 1), :].astype(
                BF16
            )

    copies = [list_copy] + near_copies + side_copies + member_copies + halo_copies + select_copies
    for copy in copies + sum_copies + x_copies:
        copy.wait_send()
    for sent in z_copies:
        for copy in sent:
            copy.wait_send()


def body(*arrays):
    arrays = list(arrays)
    for i in (6, 7):
        arrays[i] = arrays[i].T
    vmem = pl.BlockSpec(memory_space=pltpu.VMEM)
    dma = pltpu.SemaphoreType.DMA
    return pl.pallas_call(
        functools.partial(kernel, lax.axis_size("member"), lax.axis_size("space")),
        out_shape=jax.ShapeDtypeStruct((MEMBERS, CHANNELS, NODES), BF16),
        in_specs=[pl.BlockSpec(memory_space=pl.ANY)] * 12,
        out_specs=vmem,
        scratch_shapes=[
            pltpu.VMEM((MEMBERS, CHANNELS, NODES), BF16),
            pltpu.VMEM((CHANNELS, HIDDEN), BF16),
            pltpu.VMEM((1, HIDDEN, HIDDEN), BF16),
            pltpu.VMEM((1, HIDDEN, HIDDEN), BF16),
            pltpu.VMEM((1, HIDDEN, HIDDEN), BF16),
            pltpu.VMEM((1, HIDDEN), BF16),
            pltpu.VMEM((CHANNELS, HIDDEN), BF16),
            pltpu.VMEM((SLOTS, NODES), jnp.int32),
            pltpu.VMEM((2, HALO), jnp.int32),
            pltpu.VMEM((1, ENSEMBLE, HIDDEN), BF16),
            pltpu.VMEM((1, 2, HIDDEN), BF16),
            pltpu.VMEM((1, 8), jnp.int32),
            pltpu.VMEM((HIDDEN, CHANNELS), BF16),
            pltpu.VMEM((2 * HIDDEN, HIDDEN), BF16),
            pltpu.VMEM((HIDDEN, HIDDEN), BF16),
            pltpu.VMEM((HIDDEN, NODES), F32),
            pltpu.VMEM((2, HIDDEN, SLOTS * NODES), BF16),
            pltpu.VMEM((PARTS * NODES, PARTS * NODES), BF16),
            pltpu.VMEM(((PARTS + 1) * NODES, HIDDEN), BF16),
            pltpu.VMEM((2, HALO), jnp.int32),
            pltpu.VMEM((2, 1, 8), jnp.int32),
            pltpu.VMEM((MEMBERS, CHANNELS, NODES), BF16),
            pltpu.VMEM((MEMBERS // PARTS * CHANNELS, NODES), BF16),
            pltpu.VMEM((MEMBERS // PARTS * CHANNELS, NODES), BF16),
            pltpu.VMEM((MEMBERS, HIDDEN, NODES), BF16),
            pltpu.VMEM((MEMBERS, HIDDEN, NODES), F32),
            pltpu.VMEM((MEMBERS // 2, HIDDEN, NODES), BF16),
            pltpu.VMEM((2, 2, 2 * HIDDEN, SLOTS * NODES), F32),
            pltpu.VMEM((PARTS, HIDDEN, NODES), F32),
            pltpu.VMEM((2, HIDDEN, PARTS * NODES), BF16),
            pltpu.VMEM((2, MEMBERS // MEMBER_CHUNKS * CHANNELS, NODES), F32),
            pltpu.VMEM((PARTS, MEMBER_CHUNKS, 512 // MEMBER_CHUNKS, NODES), BF16),
            pltpu.VMEM((PARTS, MEMBER_CHUNKS, 512 // MEMBER_CHUNKS, NODES), BF16),
            pltpu.VMEM((PARTS, CHANNEL_CHUNKS, 512 // CHANNEL_CHUNKS, NODES), BF16),
            pltpu.VMEM((PARTS, CHANNEL_CHUNKS, 512 // CHANNEL_CHUNKS, NODES), BF16),
            pltpu.VMEM((MEMBERS * CHANNELS // CHANNEL_CHUNKS, NODES), F32),
            pltpu.VMEM((GRAM_ROWS, ENSEMBLE), F32),
            pltpu.VMEM((GRAM_ROWS, ENSEMBLE), BF16),
            pltpu.VMEM((2, GRAM_ROWS, ENSEMBLE), BF16),
            pltpu.VMEM((2, GRAM_ROWS, ENSEMBLE), BF16),
            pltpu.VMEM((2, GRAM_ROWS, ENSEMBLE), BF16),
            pltpu.VMEM((2, GRAM_ROWS, ENSEMBLE), BF16),
            dma((12,)),
            dma,
            dma,
            dma((2,)),
            dma((2,)),
            dma((MEMBER_CHUNKS,)),
            dma((MEMBER_CHUNKS,)),
            dma((MEMBER_CHUNKS,)),
            dma((MEMBER_CHUNKS,)),
            dma((2,)),
            dma((2,)),
            dma((2,)),
            dma((2,)),
            dma((2,)),
            dma((2,)),
            dma((MEMBER_CHUNKS, PARTS - 1)),
            dma((MEMBER_CHUNKS, PARTS - 1)),
            dma((CHANNEL_CHUNKS, PARTS - 1)),
            dma((CHANNEL_CHUNKS, PARTS - 1)),
        ],
        compiler_params=pltpu.CompilerParams(collective_id=0, has_side_effects=True),
        name="cycle",
    )(*arrays)


def solution(mesh):
    placed = (
        P("member", None, "space"),
        P(),
        P(),
        P(),
        P(),
        P(),
        P(),
        P("space", None),
        P(None, "space"),
        P(("member", "space"), None, None),
        P(("member", "space"), None, None),
        P(("member", "space"), None),
    )
    return jax.shard_map(
        body, mesh=mesh, in_specs=placed, out_specs=P("member", None, "space"), check_vma=False
    )
```

```python
import functools

import jax
import jax.numpy as jnp
from jax import lax
from jax.experimental import pallas as pl
from jax.experimental.pallas import tpu as pltpu
from jax.sharding import PartitionSpec as P

ITERS_NS = 5
EPSILON = 1e-05
FULL_PRECISION = lax.Precision.HIGHEST
MESH = pl.DeviceIdType.MESH
BF16 = jnp.bfloat16
F32 = jnp.float32

MEMBERS = 32
CHANNELS = 64
NODES = 128
HIDDEN = 256
HALO = 32
SLOTS = 4
PARTS = 4
ENSEMBLE = 128
GRAM_ROWS = 144
MEMBER_CHUNKS = 4
CHANNEL_CHUNKS = 4
OWN_STEP = 16


def dot(left, right):
    return jnp.dot(left, right, preferred_element_type=F32)


def dot_nt(left, right):
    return lax.dot_general(left, right, (((1,), (1,)), ((), ())), preferred_element_type=F32)


def iota(shape, dim):
    return lax.broadcasted_iota(jnp.int32, shape, dim)


def eye(extent, dtype):
    return jnp.where(iota((extent, extent), 0) == iota((extent, extent), 1), 1.0, 0.0).astype(dtype)


def split(values):
    high = values.astype(BF16)
    return high, (values - high.astype(F32)).astype(BF16)


def kernel(
    member_count,
    space_count,
    fields_hbm,
    we_hbm,
    ws_hbm,
    wr_hbm,
    wu_hbm,
    gain_hbm,
    wd_hbm,
    edge_hbm,
    halo_hbm,
    pert_hbm,
    vals_hbm,
    near_hbm,
    out_ref,
    fv,
    we_ref,
    ws_ref,
    wr_ref,
    wu_ref,
    gain_ref,
    wd_t,
    edge_ref,
    halo_ref,
    pert_ref,
    vals_ref,
    near_ref,
    we_t,
    wsr_t,
    wu_t,
    gain_col,
    pick,
    perm,
    chooser,
    lists,
    nears,
    halo_recv,
    side_send,
    side_recv,
    se,
    rv,
    sh,
    vs,
    ms,
    nb,
    fs,
    sb,
    xr,
    zs,
    zr,
    os_,
    gram_own,
    gram_send,
    gram_member,
    sum_send,
    sum_recv,
    gram_side,
    load_sem,
    list_send_sem,
    list_recv_sem,
    near_send_sem,
    near_recv_sem,
    halo_send_sem,
    halo_recv_sem,
    side_send_sem,
    side_recv_sem,
    gm_send_sem,
    gm_recv_sem,
    sum_send_sem,
    sum_recv_sem,
    gs_send_sem,
    gs_recv_sem,
    x_send_sem,
    x_recv_sem,
    z_send_sem,
    z_recv_sem,
):
    row = lax.axis_index("member")
    column = lax.axis_index("space")

    def at_member(offset):
        return (lax.rem(row + offset + member_count, member_count), column)

    def at_space(offset):
        return (row, lax.rem(column + offset + space_count, space_count))

    def remote(source, target, send_sem, recv_sem, device):
        return pltpu.make_async_remote_copy(
            src_ref=source,
            dst_ref=target,
            send_sem=send_sem,
            recv_sem=recv_sem,
            device_id=device,
            device_id_type=MESH,
        )

    barrier = pltpu.get_barrier_semaphore()
    partners = [at_space(-1)] + [at_member(d) for d in range(1, PARTS)]
    for partner in partners:
        pl.semaphore_signal(barrier, inc=1, device_id=partner, device_id_type=MESH)

    sources = (halo_hbm, near_hbm, pert_hbm, vals_hbm, we_hbm, ws_hbm, wr_hbm, fields_hbm)
    sources += (edge_hbm, wu_hbm, gain_hbm, wd_hbm)
    targets = (halo_ref, near_ref, pert_ref, vals_ref, we_ref, ws_ref, wr_ref, fv)
    targets += (edge_ref, wu_ref, gain_ref, wd_t)
    loads = [
        pltpu.make_async_copy(source, target, load_sem.at[i])
        for i, (source, target) in enumerate(zip(sources, targets))
    ]
    for load in loads:
        load.start()

    for load in (loads[0], loads[1], loads[7]):
        load.wait()
    pl.semaphore_wait(barrier, len(partners))

    list_copy = remote(halo_ref, lists, list_send_sem, list_recv_sem, at_space(1))
    near_copies = [
        remote(near_ref, nears.at[i], near_send_sem.at[i], near_recv_sem.at[i], at_space(offset))
        for i, offset in enumerate((1, -1))
    ]
    side_copies = [
        remote(gram_send, gram_side.at[i], gs_send_sem.at[i], gs_recv_sem.at[i], at_space(offset))
        for i, offset in enumerate((1, -1))
    ]
    member_copies = [
        remote(gram_send, gram_member.at[i], gm_send_sem.at[i], gm_recv_sem.at[i], at_member(offset))
        for i, offset in enumerate((1, -1))
    ]
    members = MEMBERS // MEMBER_CHUNKS
    halo_copies = []
    for chunk in range(MEMBER_CHUNKS):
        part = pl.ds(members * chunk, members)
        halo_copies.append(
            remote(
                fv.at[part],
                halo_recv.at[part],
                halo_send_sem.at[chunk],
                halo_recv_sem.at[chunk],
                at_space(1),
            )
        )
    list_copy.start()
    near_copies[0].start()
    for copy in halo_copies[0:2]:
        copy.start()

    for load in loads[2:4]:
        load.wait()
    pert = pert_ref[0]
    variance = vals_ref[0, 0:1, :].astype(F32)
    innovation = vals_ref[0, 1:2, :].astype(F32)
    scaled_high, scaled_low = split(pert.astype(F32) * variance)
    gram = dot_nt(scaled_high, pert) + dot_nt(scaled_low, pert)
    force_high, force_low = split(variance * innovation)
    sub = iota((16, HIDDEN), 0)
    force_rows = jnp.where(
        sub == 0,
        jnp.broadcast_to(force_high.astype(F32), (16, HIDDEN)),
        jnp.where(sub == 1, jnp.broadcast_to(force_low.astype(F32), (16, HIDDEN)), 0.0),
    ).astype(BF16)
    forcing = jnp.sum(dot_nt(force_rows, pert), axis=0, keepdims=True)
    sub16 = iota((16, ENSEMBLE), 0)

    def forcing_rows(values):
        high = values.astype(BF16).astype(F32)
        low = values - high
        return jnp.where(
            sub16 == 0,
            jnp.broadcast_to(high, (16, ENSEMBLE)),
            jnp.where(sub16 == 1, jnp.broadcast_to(low, (16, ENSEMBLE)), 0.0),
        )

    gram_own[0:ENSEMBLE, :] = gram
    gram_own[ENSEMBLE:GRAM_ROWS, :] = forcing_rows(forcing)
    gram_send[...] = gram_own[...].astype(BF16)

    side_copies[0].start()
    for copy in member_copies + halo_copies[2:]:
        copy.start()

    eye_hidden = eye(HIDDEN, BF16)
    repeat = jnp.where(
        iota((HALO, HIDDEN), 0) == (iota((HALO, HIDDEN), 1) & (HALO - 1)), 1.0, 0.0
    ).astype(BF16)
    lane = iota((NODES, HIDDEN), 1)
    after = ((lane >> 5) & 1) == 1


    def spread_names(values):
        values = jnp.broadcast_to(values.astype(F32), (8, HALO)).astype(BF16)
        return jnp.broadcast_to(dot(values, repeat)[0:1], (NODES, HIDDEN)).astype(jnp.int32)

    hit = spread_names(halo_ref[0:1, :]) == iota((NODES, HIDDEN), 0)
    for q in range(PARTS):
        chosen = hit & jnp.logical_not(after) & ((lane >> 6) == q)
        chooser[NODES * q : NODES * (q + 1), :] = jnp.where(chosen, 1.0, 0.0).astype(BF16)
    kept = iota((NODES, HIDDEN), 0)
    kept = (kept >> 5) * (2 * HALO) + HALO + (kept & (HALO - 1))
    chooser[PARTS * NODES :, :] = jnp.where(lane == kept, 1.0, 0.0).astype(BF16)

    for load in loads[4:7] + loads[8:]:
        load.wait()
    we_t[...] = dot_nt(eye_hidden, we_ref[...]).astype(BF16)
    wsr_t[0:HIDDEN, :] = dot_nt(eye_hidden, ws_ref[0]).astype(BF16)
    wsr_t[HIDDEN:, :] = (dot_nt(eye_hidden, wr_ref[0]) * 0.5).astype(BF16)

    groups = MEMBERS // PARTS
    for m in range(0, MEMBERS, OWN_STEP):
        wide = jnp.concatenate([fv[m + t] for t in range(OWN_STEP)], axis=1)
        rounded = dot(we_t[...], wide).astype(BF16)
        both = dot(wsr_t[...], rounded)
        for t in range(OWN_STEP):
            se[m + t] = both[0:HIDDEN, NODES * t : NODES * (t + 1)].astype(BF16)
            rv[m + t] = both[HIDDEN:, NODES * t : NODES * (t + 1)]

    wu_t[...] = dot_nt(eye_hidden, wu_ref[0]).astype(BF16)
    gain_col[...] = dot_nt(eye_hidden, jnp.broadcast_to(gain_ref[...], (NODES, HIDDEN)))
    tall = iota((HIDDEN, NODES), 0)
    for k in range(SLOTS):
        sender = jnp.broadcast_to(edge_ref[k : k + 1, :], (HIDDEN, NODES))
        for i in range(2):
            moved = sender + jnp.where(sender >= NODES, 2 * HALO * i, 0)
            hot = jnp.where(tall == moved, 0.5, 0.0).astype(BF16)
            pick[i, :, NODES * k : NODES * (k + 1)] = hot
    wide_lanes = PARTS * NODES
    r0 = iota((wide_lanes, wide_lanes), 0)
    goal = ((r0 >> 5) & 3) * NODES + (r0 >> 7) * HALO + (r0 & 31)
    perm[...] = jnp.where(iota((wide_lanes, wide_lanes), 1) == goal, 1.0, 0.0).astype(BF16)

    list_copy.wait_recv()
    near_copies[0].wait_recv()
    near_copies[1].start()
    hit = spread_names(lists[1:2, :])[:, 0:NODES] == iota((NODES, NODES), 0)
    block = iota((NODES, NODES), 1) >> 5
    wanted = jnp.concatenate(
        [jnp.where(hit & (block == q), 1.0, 0.0).astype(BF16) for q in range(PARTS)], axis=0
    )
    quads = jnp.concatenate(
        [
            jnp.concatenate([fv[PARTS * g + q] for g in range(groups)], axis=0)
            for q in range(PARTS)
        ],
        axis=1,
    )
    side_send[...] = dot(quads, wanted).astype(BF16)
    side_rows = members // PARTS * CHANNELS
    select_copies = []
    for chunk in range(MEMBER_CHUNKS):
        part = pl.ds(side_rows * chunk, side_rows)
        copy = remote(
            side_send.at[part],
            side_recv.at[part],
            side_send_sem.at[chunk],
            side_recv_sem.at[chunk],
            at_space(-1),
        )
        copy.start()
        select_copies.append(copy)
    side_copies[1].start()

    def halo(chunk):
        halo_copies[chunk].wait_recv()
        select_copies[chunk].wait_recv()
        first = members * chunk
        both = jnp.concatenate(
            [
                jnp.concatenate(
                    [halo_recv[first + PARTS * t + q] for q in range(PARTS)]
                    + [side_recv[CHANNELS * (first // PARTS + t) : CHANNELS * (first // PARTS + t + 1), :]],
                    axis=1,
                )
                for t in range(members // PARTS)
            ],
            axis=0,
        )
        ordered = dot(both, chooser[...]).astype(BF16)
        wide = jnp.concatenate(
            [ordered[CHANNELS * t : CHANNELS * (t + 1)] for t in range(members // PARTS)], axis=1
        )
        rounded = dot(we_t[...], wide).astype(BF16)
        values = dot(wsr_t[0:HIDDEN, :], rounded).astype(BF16)
        for t in range(members // 2):
            sh[first // 2 + t] = values[:, NODES * t : NODES * (t + 1)]

    def region(p, s):
        r = lax.rem(row + p + member_count, member_count)
        c = lax.rem(column + s + space_count, space_count)
        return r * space_count + c

    def weight(names, p, s, base):
        held = jnp.sum(
            jnp.where(names == region(p, base + s), 1.0, 0.0), axis=1, keepdims=True
        )
        return held * (1.0 / (1.0 + (p * p + s * s) / 2.0))

    sum_copies = []

    def send_sum(i):
        offset, s = ((1, -1), (-1, 1))[i]
        if i == 0:
            near_copies[1].wait_recv()
        side_copies[i].wait_recv()
        names = nears[1 - i]
        rows = [
            (-1, gram_member[0].astype(F32)),
            (0, gram_own[...]),
            (1, gram_member[1].astype(F32)),
        ]
        total = sum(weight(names, p, s, offset) * values for p, values in rows)
        total = total + weight(names, 0, 2 * s, offset) * gram_side[i].astype(F32)
        sum_send[i, 0:ENSEMBLE, :] = total[0:ENSEMBLE].astype(BF16)
        sum_send[i, ENSEMBLE:, :] = forcing_rows(
            jnp.sum(total[ENSEMBLE:], axis=0, keepdims=True)
        ).astype(BF16)
        copy = remote(
            sum_send.at[i], sum_recv.at[i], sum_send_sem.at[i], sum_recv_sem.at[i], at_space(offset)
        )
        copy.start()
        sum_copies.append(copy)

    for copy in member_copies:
        copy.wait_recv()
    send_sum(0)

    strip = 64
    x_copies = []

    def gather(g):
        for i in range(2):
            left = jnp.concatenate(
                [
                    jnp.concatenate([se[PARTS * g + 2 * j + i], sh[2 * g + j]], axis=1)
                    for j in range(2)
                ],
                axis=0,
            )
            vs[g % 2, i] = dot(left, pick[i])

    def message(g):
        for i in range(2):
            for j in range(2):
                q = 2 * j + i
                square = jnp.zeros((8, NODES), F32)
                for top in range(0, HIDDEN, strip):
                    base = rv[PARTS * g + q, top : top + strip, :]
                    total = None
                    for k in range(SLOTS):
                        half = (
                            vs[
                                g % 2,
                                i,
                                HIDDEN * j + top : HIDDEN * j + top + strip,
                                NODES * k : NODES * (k + 1),
                            ]
                            + base
                        )
                        term = half + half * jnp.tanh(half)
                        total = term if total is None else total + term
                    ms[q, top : top + strip, :] = total
                    squared = total * total
                    for t in range(0, strip, 8):
                        square = square + squared[t : t + 8]
                mean_square = jnp.sum(square, axis=0, keepdims=True) * (1.0 / HIDDEN)
                scale = lax.rsqrt(mean_square + EPSILON)
                for top in range(0, HIDDEN, strip):
                    nb[g % 2, top : top + strip, NODES * q : NODES * (q + 1)] = (
                        ms[q, top : top + strip, :] * scale * gain_col[top : top + strip, :]
                    ).astype(BF16)

    def update(g):
        wide = jnp.concatenate([fv[PARTS * g + q] for q in range(PARTS)], axis=1)
        final = (dot(we_t[...], wide) + dot(wu_t[...], nb[g % 2])).astype(BF16)
        values = dot(wd_t[...], final) + wide.astype(F32)
        chunk, place = divmod(PARTS * g, members)
        for q in range(PARTS):
            top = (place + q) * CHANNELS
            fs[chunk % 2, top : top + CHANNELS, :] = values[:, NODES * q : NODES * (q + 1)]
        if place + PARTS < members:
            return
        packed = jnp.concatenate(
            [
                jnp.concatenate(
                    [
                        fs[chunk % 2, pl.ds(PARTS * cg + c, members, stride=CHANNELS), :]
                        for c in range(PARTS)
                    ],
                    axis=1,
                )
                for cg in range(CHANNELS // PARTS)
            ],
            axis=0,
        ).astype(BF16)
        turned = dot(packed, perm[...]).astype(BF16)
        for target in range(PARTS):
            sb[target, chunk] = turned[:, NODES * target : NODES * (target + 1)]
        for d in range(1, PARTS):
            device = at_member(d)
            copy = remote(
                sb.at[device[0], chunk],
                xr.at[row, chunk],
                x_send_sem.at[chunk, d - 1],
                x_recv_sem.at[chunk, d - 1],
                device,
            )
            copy.start()
            x_copies.append(copy)
        xr[row, chunk] = sb[row, chunk]

    for chunk in range(MEMBER_CHUNKS):
        halo(chunk)
        first = chunk * members // PARTS
        last = first + members // PARTS
        gather(first)
        for g in range(first, last):
            if g + 1 < last:
                gather(g + 1)
            message(g)
            if g > first:
                update(g - 1)
        update(last - 1)
        if chunk == 0:
            send_sum(1)

    for copy in sum_copies:
        copy.wait_recv()
    names = near_ref[...]
    total = gram_own[...] + sum_recv[0].astype(F32) + sum_recv[1].astype(F32)
    for values, p, s in (
        (gram_member[0], -1, 0),
        (gram_member[1], 1, 0),
    ):
        total = total + weight(names, p, s, 0) * values.astype(F32)
    forcing = jnp.sum(total[ENSEMBLE:], axis=0, keepdims=True)
    identity = eye(ENSEMBLE, F32)
    system = identity + total[0:ENSEMBLE] / (ENSEMBLE - 1)
    norm = jnp.sum(jnp.sum(system * system, axis=1, keepdims=True), axis=0, keepdims=True)
    scaling = jnp.sqrt(norm)
    iterate = system / scaling
    inverse = identity

    def full(left, right):
        return jnp.dot(left, right, precision=FULL_PRECISION, preferred_element_type=F32)

    for _ in range(ITERS_NS):
        correction = 1.5 * identity - 0.5 * full(inverse, iterate)
        iterate = full(iterate, correction)
        inverse = full(correction, inverse)
    forcing = jnp.broadcast_to(forcing, (8, ENSEMBLE))
    mean_weights = full(full(forcing, inverse), inverse)[0:1] / (scaling * (ENSEMBLE - 1))
    root = inverse / jnp.sqrt(scaling)
    rest = (
        1.0
        - jnp.sum(root, axis=1, keepdims=True)
        - jnp.sum(mean_weights, axis=1, keepdims=True)
    ) * (1.0 / ENSEMBLE)
    lane = iota((ENSEMBLE, 2 * ENSEMBLE), 1)
    source = iota((ENSEMBLE, 2 * ENSEMBLE), 0)
    same = ((lane >> 4) == (source >> 3)) & ((lane & 7) == (source & 7))
    spread = [
        jnp.where(same & (((lane >> 3) & 1) == half), 1.0, 0.0).astype(BF16) for half in range(2)
    ]
    mix_high, mix_low = [
        jnp.concatenate([dot(part, s) for s in spread], axis=0).astype(BF16)
        for part in split(root + mean_weights + rest)
    ]

    for copy in x_copies:
        copy.wait_recv()
    per_chunk = CHANNELS // PARTS // CHANNEL_CHUNKS
    owned = MEMBERS
    z_copies = []
    for ch in range(CHANNEL_CHUNKS):
        states = jnp.concatenate(
            [
                jnp.concatenate(
                    [
                        xr[source, chunk, 16 * pair : 16 * (pair + 1), :]
                        for source in range(PARTS)
                        for chunk in range(MEMBER_CHUNKS)
                    ],
                    axis=0,
                )
                for pair in range(ch * per_chunk // 2, (ch + 1) * per_chunk // 2)
            ],
            axis=1,
        )
        mixed = (dot(mix_high, states) + dot(mix_low, states)).astype(BF16)
        for target in range(PARTS):
            for cg in range(per_chunk):
                top = ENSEMBLE * (cg % 2) + owned * target
                zs[target, ch, owned * cg : owned * (cg + 1), :] = mixed[
                    top : top + owned, NODES * (cg // 2) : NODES * (cg // 2 + 1)
                ]
        sent = []
        for d in range(1, PARTS):
            device = at_member(d)
            copy = remote(
                zs.at[device[0], ch],
                zr.at[row, ch],
                z_send_sem.at[ch, d - 1],
                z_recv_sem.at[ch, d - 1],
                device,
            )
            copy.start()
            sent.append(copy)
        z_copies.append(sent)
        zr[row, ch] = zs[row, ch]

    span = PARTS * per_chunk
    for ch in range(CHANNEL_CHUNKS):
        for copy in z_copies[ch]:
            copy.wait_recv()
        packed = jnp.concatenate([zr[source, ch] for source in range(PARTS)], axis=1)
        turned = dot(packed, perm[...])
        for cg in range(per_chunk):
            for c in range(PARTS):
                os_[pl.ds(PARTS * cg + c, owned, stride=span), :] = turned[
                    owned * cg : owned * (cg + 1), NODES * c : NODES * (c + 1)
                ]
        for j in range(owned):
            out_ref[j, span * ch : span * (ch + 1), :] = os_[span * j : span * (j + 1), :].astype(
                BF16
            )

    copies = [list_copy] + near_copies + side_copies + member_copies + halo_copies + select_copies
    for copy in copies + sum_copies + x_copies:
        copy.wait_send()
    for sent in z_copies:
        for copy in sent:
            copy.wait_send()


def body(*arrays):
    arrays = list(arrays)
    for i in (6, 7):
        arrays[i] = arrays[i].T
    vmem = pl.BlockSpec(memory_space=pltpu.VMEM)
    dma = pltpu.SemaphoreType.DMA
    result = pl.pallas_call(
        functools.partial(kernel, lax.axis_size("member"), lax.axis_size("space")),
        out_shape=pltpu.VMEM((MEMBERS, CHANNELS, NODES), BF16),
        in_specs=[pl.BlockSpec(memory_space=pl.ANY)] * 12,
        out_specs=vmem,
        scratch_shapes=[
            pltpu.VMEM((MEMBERS, CHANNELS, NODES), BF16),
            pltpu.VMEM((CHANNELS, HIDDEN), BF16),
            pltpu.VMEM((1, HIDDEN, HIDDEN), BF16),
            pltpu.VMEM((1, HIDDEN, HIDDEN), BF16),
            pltpu.VMEM((1, HIDDEN, HIDDEN), BF16),
            pltpu.VMEM((1, HIDDEN), BF16),
            pltpu.VMEM((CHANNELS, HIDDEN), BF16),
            pltpu.VMEM((SLOTS, NODES), jnp.int32),
            pltpu.VMEM((2, HALO), jnp.int32),
            pltpu.VMEM((1, ENSEMBLE, HIDDEN), BF16),
            pltpu.VMEM((1, 2, HIDDEN), BF16),
            pltpu.VMEM((1, 8), jnp.int32),
            pltpu.VMEM((HIDDEN, CHANNELS), BF16),
            pltpu.VMEM((2 * HIDDEN, HIDDEN), BF16),
            pltpu.VMEM((HIDDEN, HIDDEN), BF16),
            pltpu.VMEM((HIDDEN, NODES), F32),
            pltpu.VMEM((2, HIDDEN, SLOTS * NODES), BF16),
            pltpu.VMEM((PARTS * NODES, PARTS * NODES), BF16),
            pltpu.VMEM(((PARTS + 1) * NODES, HIDDEN), BF16),
            pltpu.VMEM((2, HALO), jnp.int32),
            pltpu.VMEM((2, 1, 8), jnp.int32),
            pltpu.VMEM((MEMBERS, CHANNELS, NODES), BF16),
            pltpu.VMEM((MEMBERS // PARTS * CHANNELS, NODES), BF16),
            pltpu.VMEM((MEMBERS // PARTS * CHANNELS, NODES), BF16),
            pltpu.VMEM((MEMBERS, HIDDEN, NODES), BF16),
            pltpu.VMEM((MEMBERS, HIDDEN, NODES), F32),
            pltpu.VMEM((MEMBERS // 2, HIDDEN, NODES), BF16),
            pltpu.VMEM((2, 2, 2 * HIDDEN, SLOTS * NODES), F32),
            pltpu.VMEM((PARTS, HIDDEN, NODES), F32),
            pltpu.VMEM((2, HIDDEN, PARTS * NODES), BF16),
            pltpu.VMEM((2, MEMBERS // MEMBER_CHUNKS * CHANNELS, NODES), F32),
            pltpu.VMEM((PARTS, MEMBER_CHUNKS, 512 // MEMBER_CHUNKS, NODES), BF16),
            pltpu.VMEM((PARTS, MEMBER_CHUNKS, 512 // MEMBER_CHUNKS, NODES), BF16),
            pltpu.VMEM((PARTS, CHANNEL_CHUNKS, 512 // CHANNEL_CHUNKS, NODES), BF16),
            pltpu.VMEM((PARTS, CHANNEL_CHUNKS, 512 // CHANNEL_CHUNKS, NODES), BF16),
            pltpu.VMEM((MEMBERS * CHANNELS // CHANNEL_CHUNKS, NODES), F32),
            pltpu.VMEM((GRAM_ROWS, ENSEMBLE), F32),
            pltpu.VMEM((GRAM_ROWS, ENSEMBLE), BF16),
            pltpu.VMEM((2, GRAM_ROWS, ENSEMBLE), BF16),
            pltpu.VMEM((2, GRAM_ROWS, ENSEMBLE), BF16),
            pltpu.VMEM((2, GRAM_ROWS, ENSEMBLE), BF16),
            pltpu.VMEM((2, GRAM_ROWS, ENSEMBLE), BF16),
            dma((12,)),
            dma,
            dma,
            dma((2,)),
            dma((2,)),
            dma((MEMBER_CHUNKS,)),
            dma((MEMBER_CHUNKS,)),
            dma((MEMBER_CHUNKS,)),
            dma((MEMBER_CHUNKS,)),
            dma((2,)),
            dma((2,)),
            dma((2,)),
            dma((2,)),
            dma((2,)),
            dma((2,)),
            dma((MEMBER_CHUNKS, PARTS - 1)),
            dma((MEMBER_CHUNKS, PARTS - 1)),
            dma((CHANNEL_CHUNKS, PARTS - 1)),
            dma((CHANNEL_CHUNKS, PARTS - 1)),
        ],
        compiler_params=pltpu.CompilerParams(collective_id=0, has_side_effects=True),
        name="cycle",
    )(*arrays)

    def hand_on(source, target, sem):
        copy = pltpu.make_async_copy(source, target, sem)
        copy.start()
        copy.wait()

    return pl.pallas_call(
        hand_on,
        out_shape=jax.ShapeDtypeStruct((MEMBERS, CHANNELS, NODES), BF16),
        in_specs=[vmem],
        out_specs=pl.BlockSpec(memory_space=pl.ANY),
        scratch_shapes=[dma],
        name="hand_on",
    )(pltpu.with_memory_space_constraint(result, pltpu.VMEM))


def solution(mesh):
    placed = (
        P("member", None, "space"),
        P(),
        P(),
        P(),
        P(),
        P(),
        P(),
        P("space", None),
        P(None, "space"),
        P(("member", "space"), None, None),
        P(("member", "space"), None, None),
        P(("member", "space"), None),
    )
    return jax.shard_map(
        body, mesh=mesh, in_specs=placed, out_specs=P("member", None, "space"), check_vma=False
    )
```

```python
import functools

import jax
import jax.numpy as jnp
from jax import lax
from jax.experimental import pallas as pl
from jax.experimental.pallas import tpu as pltpu
from jax.sharding import PartitionSpec as P

ITERS_NS = 5
EPSILON = 1e-05
FULL_PRECISION = lax.Precision.HIGHEST
MESH = pl.DeviceIdType.MESH
BF16 = jnp.bfloat16
F32 = jnp.float32

MEMBERS = 32
CHANNELS = 64
NODES = 128
HIDDEN = 256
HALO = 32
SLOTS = 4
PARTS = 4
ENSEMBLE = 128
GRAM_ROWS = 144
MEMBER_CHUNKS = 4
CHANNEL_CHUNKS = 4
OWN_STEP = 16


def dot(left, right):
    return jnp.dot(left, right, preferred_element_type=F32)


def dot_nt(left, right):
    return lax.dot_general(left, right, (((1,), (1,)), ((), ())), preferred_element_type=F32)


def iota(shape, dim):
    return lax.broadcasted_iota(jnp.int32, shape, dim)


def eye(extent, dtype):
    return jnp.where(iota((extent, extent), 0) == iota((extent, extent), 1), 1.0, 0.0).astype(dtype)


def split(values):
    high = values.astype(BF16)
    return high, (values - high.astype(F32)).astype(BF16)


def kernel(
    member_count,
    space_count,
    fields_hbm,
    we_hbm,
    ws_hbm,
    wr_hbm,
    wu_hbm,
    gain_hbm,
    wd_hbm,
    edge_hbm,
    halo_hbm,
    pert_hbm,
    vals_hbm,
    near_hbm,
    out_ref,
    fv,
    we_ref,
    ws_ref,
    wr_ref,
    wu_ref,
    gain_ref,
    wd_t,
    edge_ref,
    halo_ref,
    pert_ref,
    vals_ref,
    near_ref,
    we_t,
    wsr_t,
    wu_t,
    gain_col,
    pick,
    perm,
    chooser,
    lists,
    nears,
    halo_recv,
    side_send,
    side_recv,
    se,
    rv,
    sh,
    vs,
    ms,
    nb,
    fs,
    sb,
    xr,
    zs,
    zr,
    os_,
    gram_own,
    gram_send,
    gram_member,
    sum_send,
    sum_recv,
    gram_side,
    load_sem,
    list_send_sem,
    list_recv_sem,
    near_send_sem,
    near_recv_sem,
    halo_send_sem,
    halo_recv_sem,
    side_send_sem,
    side_recv_sem,
    gm_send_sem,
    gm_recv_sem,
    sum_send_sem,
    sum_recv_sem,
    gs_send_sem,
    gs_recv_sem,
    x_send_sem,
    x_recv_sem,
    z_send_sem,
    z_recv_sem,
):
    row = lax.axis_index("member")
    column = lax.axis_index("space")

    def at_member(offset):
        return (lax.rem(row + offset + member_count, member_count), column)

    def at_space(offset):
        return (row, lax.rem(column + offset + space_count, space_count))

    def remote(source, target, send_sem, recv_sem, device):
        return pltpu.make_async_remote_copy(
            src_ref=source,
            dst_ref=target,
            send_sem=send_sem,
            recv_sem=recv_sem,
            device_id=device,
            device_id_type=MESH,
        )

    barrier = pltpu.get_barrier_semaphore()
    partners = [at_space(-1)] + [at_member(d) for d in range(1, PARTS)]
    for partner in partners:
        pl.semaphore_signal(barrier, inc=1, device_id=partner, device_id_type=MESH)

    sources = (halo_hbm, near_hbm, pert_hbm, vals_hbm, we_hbm, ws_hbm, wr_hbm, fields_hbm)
    sources += (edge_hbm, wu_hbm, gain_hbm, wd_hbm)
    targets = (halo_ref, near_ref, pert_ref, vals_ref, we_ref, ws_ref, wr_ref, fv)
    targets += (edge_ref, wu_ref, gain_ref, wd_t)
    loads = [
        pltpu.make_async_copy(source, target, load_sem.at[i])
        for i, (source, target) in enumerate(zip(sources, targets))
    ]
    for load in loads:
        load.start()

    for load in loads[2:4]:
        load.wait()
    pert = pert_ref[0]
    variance = vals_ref[0, 0:1, :].astype(F32)
    innovation = vals_ref[0, 1:2, :].astype(F32)
    scaled_high, scaled_low = split(pert.astype(F32) * variance)
    gram = dot_nt(scaled_high, pert) + dot_nt(scaled_low, pert)
    force_high, force_low = split(variance * innovation)
    sub = iota((16, HIDDEN), 0)
    force_rows = jnp.where(
        sub == 0,
        jnp.broadcast_to(force_high.astype(F32), (16, HIDDEN)),
        jnp.where(sub == 1, jnp.broadcast_to(force_low.astype(F32), (16, HIDDEN)), 0.0),
    ).astype(BF16)
    forcing = jnp.sum(dot_nt(force_rows, pert), axis=0, keepdims=True)
    sub16 = iota((16, ENSEMBLE), 0)

    def forcing_rows(values):
        high = values.astype(BF16).astype(F32)
        low = values - high
        return jnp.where(
            sub16 == 0,
            jnp.broadcast_to(high, (16, ENSEMBLE)),
            jnp.where(sub16 == 1, jnp.broadcast_to(low, (16, ENSEMBLE)), 0.0),
        )

    gram_own[0:ENSEMBLE, :] = gram
    gram_own[ENSEMBLE:GRAM_ROWS, :] = forcing_rows(forcing)
    gram_send[...] = gram_own[...].astype(BF16)

    for load in (loads[0], loads[1], loads[7]):
        load.wait()
    pl.semaphore_wait(barrier, len(partners))

    list_copy = remote(halo_ref, lists, list_send_sem, list_recv_sem, at_space(1))
    near_copies = [
        remote(near_ref, nears.at[i], near_send_sem.at[i], near_recv_sem.at[i], at_space(offset))
        for i, offset in enumerate((1, -1))
    ]
    side_copies = [
        remote(gram_send, gram_side.at[i], gs_send_sem.at[i], gs_recv_sem.at[i], at_space(offset))
        for i, offset in enumerate((1, -1))
    ]
    member_copies = [
        remote(gram_send, gram_member.at[i], gm_send_sem.at[i], gm_recv_sem.at[i], at_member(offset))
        for i, offset in enumerate((1, -1))
    ]
    members = MEMBERS // MEMBER_CHUNKS
    halo_copies = []
    for chunk in range(MEMBER_CHUNKS):
        part = pl.ds(members * chunk, members)
        halo_copies.append(
            remote(
                fv.at[part],
                halo_recv.at[part],
                halo_send_sem.at[chunk],
                halo_recv_sem.at[chunk],
                at_space(1),
            )
        )
    list_copy.start()
    near_copies[0].start()
    side_copies[0].start()
    for copy in halo_copies[0:2]:
        copy.start()

    for copy in member_copies:
        copy.start()

    eye_hidden = eye(HIDDEN, BF16)
    repeat = jnp.where(
        iota((HALO, HIDDEN), 0) == (iota((HALO, HIDDEN), 1) & (HALO - 1)), 1.0, 0.0
    ).astype(BF16)
    lane = iota((NODES, HIDDEN), 1)
    after = ((lane >> 5) & 1) == 1


    def spread_names(values):
        values = jnp.broadcast_to(values.astype(F32), (8, HALO)).astype(BF16)
        return jnp.broadcast_to(dot(values, repeat)[0:1], (NODES, HIDDEN)).astype(jnp.int32)

    hit = spread_names(halo_ref[0:1, :]) == iota((NODES, HIDDEN), 0)
    for q in range(PARTS):
        chosen = hit & jnp.logical_not(after) & ((lane >> 6) == q)
        chooser[NODES * q : NODES * (q + 1), :] = jnp.where(chosen, 1.0, 0.0).astype(BF16)
    kept = iota((NODES, HIDDEN), 0)
    kept = (kept >> 5) * (2 * HALO) + HALO + (kept & (HALO - 1))
    chooser[PARTS * NODES :, :] = jnp.where(lane == kept, 1.0, 0.0).astype(BF16)

    for load in loads[4:7] + loads[8:]:
        load.wait()
    halo_copies[0].wait_send()
    halo_copies[2].start()

    we_t[...] = dot_nt(eye_hidden, we_ref[...]).astype(BF16)
    wsr_t[0:HIDDEN, :] = dot_nt(eye_hidden, ws_ref[0]).astype(BF16)
    wsr_t[HIDDEN:, :] = (dot_nt(eye_hidden, wr_ref[0]) * 0.5).astype(BF16)

    groups = MEMBERS // PARTS
    for m in range(0, MEMBERS, OWN_STEP):
        wide = jnp.concatenate([fv[m + t] for t in range(OWN_STEP)], axis=1)
        rounded = dot(we_t[...], wide).astype(BF16)
        both = dot(wsr_t[...], rounded)
        for t in range(OWN_STEP):
            se[m + t] = both[0:HIDDEN, NODES * t : NODES * (t + 1)].astype(BF16)
            rv[m + t] = both[HIDDEN:, NODES * t : NODES * (t + 1)]

    halo_copies[1].wait_send()
    halo_copies[3].start()
    wu_t[...] = dot_nt(eye_hidden, wu_ref[0]).astype(BF16)
    gain_col[...] = dot_nt(eye_hidden, jnp.broadcast_to(gain_ref[...], (NODES, HIDDEN)))
    tall = iota((HIDDEN, NODES), 0)
    for k in range(SLOTS):
        sender = jnp.broadcast_to(edge_ref[k : k + 1, :], (HIDDEN, NODES))
        for i in range(2):
            moved = sender + jnp.where(sender >= NODES, 2 * HALO * i, 0)
            hot = jnp.where(tall == moved, 0.5, 0.0).astype(BF16)
            pick[i, :, NODES * k : NODES * (k + 1)] = hot
    wide_lanes = PARTS * NODES
    r0 = iota((wide_lanes, wide_lanes), 0)
    goal = ((r0 >> 5) & 3) * NODES + (r0 >> 7) * HALO + (r0 & 31)
    perm[...] = jnp.where(iota((wide_lanes, wide_lanes), 1) == goal, 1.0, 0.0).astype(BF16)

    list_copy.wait_recv()
    near_copies[0].wait_recv()
    near_copies[1].start()
    hit = spread_names(lists[1:2, :])[:, 0:NODES] == iota((NODES, NODES), 0)
    block = iota((NODES, NODES), 1) >> 5
    wanted = jnp.concatenate(
        [jnp.where(hit & (block == q), 1.0, 0.0).astype(BF16) for q in range(PARTS)], axis=0
    )
    quads = jnp.concatenate(
        [
            jnp.concatenate([fv[PARTS * g + q] for g in range(groups)], axis=0)
            for q in range(PARTS)
        ],
        axis=1,
    )
    side_send[...] = dot(quads, wanted).astype(BF16)
    side_rows = members // PARTS * CHANNELS
    select_copies = []
    for chunk in range(MEMBER_CHUNKS):
        part = pl.ds(side_rows * chunk, side_rows)
        copy = remote(
            side_send.at[part],
            side_recv.at[part],
            side_send_sem.at[chunk],
            side_recv_sem.at[chunk],
            at_space(-1),
        )
        copy.start()
        select_copies.append(copy)
    side_copies[1].start()

    def halo(chunk):
        halo_copies[chunk].wait_recv()
        select_copies[chunk].wait_recv()
        first = members * chunk
        both = jnp.concatenate(
            [
                jnp.concatenate(
                    [halo_recv[first + PARTS * t + q] for q in range(PARTS)]
                    + [side_recv[CHANNELS * (first // PARTS + t) : CHANNELS * (first // PARTS + t + 1), :]],
                    axis=1,
                )
                for t in range(members // PARTS)
            ],
            axis=0,
        )
        ordered = dot(both, chooser[...]).astype(BF16)
        wide = jnp.concatenate(
            [ordered[CHANNELS * t : CHANNELS * (t + 1)] for t in range(members // PARTS)], axis=1
        )
        rounded = dot(we_t[...], wide).astype(BF16)
        values = dot(wsr_t[0:HIDDEN, :], rounded).astype(BF16)
        for t in range(members // 2):
            sh[first // 2 + t] = values[:, NODES * t : NODES * (t + 1)]

    def region(p, s):
        r = lax.rem(row + p + member_count, member_count)
        c = lax.rem(column + s + space_count, space_count)
        return r * space_count + c

    def weight(names, p, s, base):
        held = jnp.sum(
            jnp.where(names == region(p, base + s), 1.0, 0.0), axis=1, keepdims=True
        )
        return held * (1.0 / (1.0 + (p * p + s * s) / 2.0))

    sum_copies = []

    def send_sum(i):
        offset, s = ((1, -1), (-1, 1))[i]
        if i == 0:
            near_copies[1].wait_recv()
        side_copies[i].wait_recv()
        names = nears[1 - i]
        rows = [
            (-1, gram_member[0].astype(F32)),
            (0, gram_own[...]),
            (1, gram_member[1].astype(F32)),
        ]
        total = sum(weight(names, p, s, offset) * values for p, values in rows)
        total = total + weight(names, 0, 2 * s, offset) * gram_side[i].astype(F32)
        sum_send[i, 0:ENSEMBLE, :] = total[0:ENSEMBLE].astype(BF16)
        sum_send[i, ENSEMBLE:, :] = forcing_rows(
            jnp.sum(total[ENSEMBLE:], axis=0, keepdims=True)
        ).astype(BF16)
        copy = remote(
            sum_send.at[i], sum_recv.at[i], sum_send_sem.at[i], sum_recv_sem.at[i], at_space(offset)
        )
        copy.start()
        sum_copies.append(copy)

    for copy in member_copies:
        copy.wait_recv()
    send_sum(0)

    strip = 64
    x_copies = []

    def gather(g):
        for i in range(2):
            left = jnp.concatenate(
                [
                    jnp.concatenate([se[PARTS * g + 2 * j + i], sh[2 * g + j]], axis=1)
                    for j in range(2)
                ],
                axis=0,
            )
            vs[g % 2, i] = dot(left, pick[i])

    def message(g):
        for i in range(2):
            for j in range(2):
                q = 2 * j + i
                square = jnp.zeros((8, NODES), F32)
                for top in range(0, HIDDEN, strip):
                    base = rv[PARTS * g + q, top : top + strip, :]
                    total = None
                    for k in range(SLOTS):
                        half = (
                            vs[
                                g % 2,
                                i,
                                HIDDEN * j + top : HIDDEN * j + top + strip,
                                NODES * k : NODES * (k + 1),
                            ]
                            + base
                        )
                        term = half + half * jnp.tanh(half)
                        total = term if total is None else total + term
                    ms[q, top : top + strip, :] = total
                    squared = total * total
                    for t in range(0, strip, 8):
                        square = square + squared[t : t + 8]
                mean_square = jnp.sum(square, axis=0, keepdims=True) * (1.0 / HIDDEN)
                scale = lax.rsqrt(mean_square + EPSILON)
                for top in range(0, HIDDEN, strip):
                    nb[g % 2, top : top + strip, NODES * q : NODES * (q + 1)] = (
                        ms[q, top : top + strip, :] * scale * gain_col[top : top + strip, :]
                    ).astype(BF16)

    def update(g):
        wide = jnp.concatenate([fv[PARTS * g + q] for q in range(PARTS)], axis=1)
        final = (dot(we_t[...], wide) + dot(wu_t[...], nb[g % 2])).astype(BF16)
        values = dot(wd_t[...], final) + wide.astype(F32)
        chunk, place = divmod(PARTS * g, members)
        for q in range(PARTS):
            top = (place + q) * CHANNELS
            fs[chunk % 2, top : top + CHANNELS, :] = values[:, NODES * q : NODES * (q + 1)]
        if place + PARTS < members:
            return
        packed = jnp.concatenate(
            [
                jnp.concatenate(
                    [
                        fs[chunk % 2, pl.ds(PARTS * cg + c, members, stride=CHANNELS), :]
                        for c in range(PARTS)
                    ],
                    axis=1,
                )
                for cg in range(CHANNELS // PARTS)
            ],
            axis=0,
        ).astype(BF16)
        turned = dot(packed, perm[...]).astype(BF16)
        for target in range(PARTS):
            sb[target, chunk] = turned[:, NODES * target : NODES * (target + 1)]
        for d in range(1, PARTS):
            device = at_member(d)
            copy = remote(
                sb.at[device[0], chunk],
                xr.at[row, chunk],
                x_send_sem.at[chunk, d - 1],
                x_recv_sem.at[chunk, d - 1],
                device,
            )
            copy.start()
            x_copies.append(copy)
        xr[row, chunk] = sb[row, chunk]

    for chunk in range(MEMBER_CHUNKS):
        halo(chunk)
        first = chunk * members // PARTS
        last = first + members // PARTS
        gather(first)
        for g in range(first, last):
            if g + 1 < last:
                gather(g + 1)
            message(g)
            if g > first:
                update(g - 1)
        update(last - 1)
        if chunk == 0:
            send_sum(1)

    for copy in sum_copies:
        copy.wait_recv()
    names = near_ref[...]
    total = gram_own[...] + sum_recv[0].astype(F32) + sum_recv[1].astype(F32)
    for values, p, s in (
        (gram_member[0], -1, 0),
        (gram_member[1], 1, 0),
    ):
        total = total + weight(names, p, s, 0) * values.astype(F32)
    forcing = jnp.sum(total[ENSEMBLE:], axis=0, keepdims=True)
    identity = eye(ENSEMBLE, F32)
    system = identity + total[0:ENSEMBLE] / (ENSEMBLE - 1)
    norm = jnp.sum(jnp.sum(system * system, axis=1, keepdims=True), axis=0, keepdims=True)
    scaling = jnp.sqrt(norm)
    iterate = system / scaling
    inverse = identity

    def full(left, right):
        return jnp.dot(left, right, precision=FULL_PRECISION, preferred_element_type=F32)

    for _ in range(ITERS_NS):
        correction = 1.5 * identity - 0.5 * full(inverse, iterate)
        iterate = full(iterate, correction)
        inverse = full(correction, inverse)
    forcing = jnp.broadcast_to(forcing, (8, ENSEMBLE))
    mean_weights = full(full(forcing, inverse), inverse)[0:1] / (scaling * (ENSEMBLE - 1))
    root = inverse / jnp.sqrt(scaling)
    rest = (
        1.0
        - jnp.sum(root, axis=1, keepdims=True)
        - jnp.sum(mean_weights, axis=1, keepdims=True)
    ) * (1.0 / ENSEMBLE)
    lane = iota((ENSEMBLE, 2 * ENSEMBLE), 1)
    source = iota((ENSEMBLE, 2 * ENSEMBLE), 0)
    same = ((lane >> 4) == (source >> 3)) & ((lane & 7) == (source & 7))
    spread = [
        jnp.where(same & (((lane >> 3) & 1) == half), 1.0, 0.0).astype(BF16) for half in range(2)
    ]
    mix_high, mix_low = [
        jnp.concatenate([dot(part, s) for s in spread], axis=0).astype(BF16)
        for part in split(root + mean_weights + rest)
    ]

    for copy in x_copies:
        copy.wait_recv()
    per_chunk = CHANNELS // PARTS // CHANNEL_CHUNKS
    owned = MEMBERS
    z_copies = []
    for ch in range(CHANNEL_CHUNKS):
        states = jnp.concatenate(
            [
                jnp.concatenate(
                    [
                        xr[source, chunk, 16 * pair : 16 * (pair + 1), :]
                        for source in range(PARTS)
                        for chunk in range(MEMBER_CHUNKS)
                    ],
                    axis=0,
                )
                for pair in range(ch * per_chunk // 2, (ch + 1) * per_chunk // 2)
            ],
            axis=1,
        )
        mixed = (dot(mix_high, states) + dot(mix_low, states)).astype(BF16)
        for target in range(PARTS):
            for cg in range(per_chunk):
                top = ENSEMBLE * (cg % 2) + owned * target
                zs[target, ch, owned * cg : owned * (cg + 1), :] = mixed[
                    top : top + owned, NODES * (cg // 2) : NODES * (cg // 2 + 1)
                ]
        sent = []
        for d in range(1, PARTS):
            device = at_member(d)
            copy = remote(
                zs.at[device[0], ch],
                zr.at[row, ch],
                z_send_sem.at[ch, d - 1],
                z_recv_sem.at[ch, d - 1],
                device,
            )
            copy.start()
            sent.append(copy)
        z_copies.append(sent)
        zr[row, ch] = zs[row, ch]

    span = PARTS * per_chunk
    for ch in range(CHANNEL_CHUNKS):
        for copy in z_copies[ch]:
            copy.wait_recv()
        packed = jnp.concatenate([zr[source, ch] for source in range(PARTS)], axis=1)
        turned = dot(packed, perm[...])
        for cg in range(per_chunk):
            for c in range(PARTS):
                os_[pl.ds(PARTS * cg + c, owned, stride=span), :] = turned[
                    owned * cg : owned * (cg + 1), NODES * c : NODES * (c + 1)
                ]
        for j in range(owned):
            out_ref[j, span * ch : span * (ch + 1), :] = os_[span * j : span * (j + 1), :].astype(
                BF16
            )

    copies = [list_copy] + near_copies + side_copies + member_copies + halo_copies[2:] + select_copies
    for copy in copies + sum_copies + x_copies:
        copy.wait_send()
    for sent in z_copies:
        for copy in sent:
            copy.wait_send()


def body(*arrays):
    arrays = list(arrays)
    for i in (6, 7):
        arrays[i] = arrays[i].T
    vmem = pl.BlockSpec(memory_space=pltpu.VMEM)
    dma = pltpu.SemaphoreType.DMA
    result = pl.pallas_call(
        functools.partial(kernel, lax.axis_size("member"), lax.axis_size("space")),
        out_shape=pltpu.VMEM((MEMBERS, CHANNELS, NODES), BF16),
        in_specs=[pl.BlockSpec(memory_space=pl.ANY)] * 12,
        out_specs=vmem,
        scratch_shapes=[
            pltpu.VMEM((MEMBERS, CHANNELS, NODES), BF16),
            pltpu.VMEM((CHANNELS, HIDDEN), BF16),
            pltpu.VMEM((1, HIDDEN, HIDDEN), BF16),
            pltpu.VMEM((1, HIDDEN, HIDDEN), BF16),
            pltpu.VMEM((1, HIDDEN, HIDDEN), BF16),
            pltpu.VMEM((1, HIDDEN), BF16),
            pltpu.VMEM((CHANNELS, HIDDEN), BF16),
            pltpu.VMEM((SLOTS, NODES), jnp.int32),
            pltpu.VMEM((2, HALO), jnp.int32),
            pltpu.VMEM((1, ENSEMBLE, HIDDEN), BF16),
            pltpu.VMEM((1, 2, HIDDEN), BF16),
            pltpu.VMEM((1, 8), jnp.int32),
            pltpu.VMEM((HIDDEN, CHANNELS), BF16),
            pltpu.VMEM((2 * HIDDEN, HIDDEN), BF16),
            pltpu.VMEM((HIDDEN, HIDDEN), BF16),
            pltpu.VMEM((HIDDEN, NODES), F32),
            pltpu.VMEM((2, HIDDEN, SLOTS * NODES), BF16),
            pltpu.VMEM((PARTS * NODES, PARTS * NODES), BF16),
            pltpu.VMEM(((PARTS + 1) * NODES, HIDDEN), BF16),
            pltpu.VMEM((2, HALO), jnp.int32),
            pltpu.VMEM((2, 1, 8), jnp.int32),
            pltpu.VMEM((MEMBERS, CHANNELS, NODES), BF16),
            pltpu.VMEM((MEMBERS // PARTS * CHANNELS, NODES), BF16),
            pltpu.VMEM((MEMBERS // PARTS * CHANNELS, NODES), BF16),
            pltpu.VMEM((MEMBERS, HIDDEN, NODES), BF16),
            pltpu.VMEM((MEMBERS, HIDDEN, NODES), F32),
            pltpu.VMEM((MEMBERS // 2, HIDDEN, NODES), BF16),
            pltpu.VMEM((2, 2, 2 * HIDDEN, SLOTS * NODES), F32),
            pltpu.VMEM((PARTS, HIDDEN, NODES), F32),
            pltpu.VMEM((2, HIDDEN, PARTS * NODES), BF16),
            pltpu.VMEM((2, MEMBERS // MEMBER_CHUNKS * CHANNELS, NODES), F32),
            pltpu.VMEM((PARTS, MEMBER_CHUNKS, 512 // MEMBER_CHUNKS, NODES), BF16),
            pltpu.VMEM((PARTS, MEMBER_CHUNKS, 512 // MEMBER_CHUNKS, NODES), BF16),
            pltpu.VMEM((PARTS, CHANNEL_CHUNKS, 512 // CHANNEL_CHUNKS, NODES), BF16),
            pltpu.VMEM((PARTS, CHANNEL_CHUNKS, 512 // CHANNEL_CHUNKS, NODES), BF16),
            pltpu.VMEM((MEMBERS * CHANNELS // CHANNEL_CHUNKS, NODES), F32),
            pltpu.VMEM((GRAM_ROWS, ENSEMBLE), F32),
            pltpu.VMEM((GRAM_ROWS, ENSEMBLE), BF16),
            pltpu.VMEM((2, GRAM_ROWS, ENSEMBLE), BF16),
            pltpu.VMEM((2, GRAM_ROWS, ENSEMBLE), BF16),
            pltpu.VMEM((2, GRAM_ROWS, ENSEMBLE), BF16),
            pltpu.VMEM((2, GRAM_ROWS, ENSEMBLE), BF16),
            dma((12,)),
            dma,
            dma,
            dma((2,)),
            dma((2,)),
            dma((MEMBER_CHUNKS,)),
            dma((MEMBER_CHUNKS,)),
            dma((MEMBER_CHUNKS,)),
            dma((MEMBER_CHUNKS,)),
            dma((2,)),
            dma((2,)),
            dma((2,)),
            dma((2,)),
            dma((2,)),
            dma((2,)),
            dma((MEMBER_CHUNKS, PARTS - 1)),
            dma((MEMBER_CHUNKS, PARTS - 1)),
            dma((CHANNEL_CHUNKS, PARTS - 1)),
            dma((CHANNEL_CHUNKS, PARTS - 1)),
        ],
        compiler_params=pltpu.CompilerParams(collective_id=0, has_side_effects=True),
        name="cycle",
    )(*arrays)

    def hand_on(source, target, sem):
        copy = pltpu.make_async_copy(source, target, sem)
        copy.start()
        copy.wait()

    return pl.pallas_call(
        hand_on,
        out_shape=jax.ShapeDtypeStruct((MEMBERS, CHANNELS, NODES), BF16),
        in_specs=[vmem],
        out_specs=pl.BlockSpec(memory_space=pl.ANY),
        scratch_shapes=[dma],
        name="hand_on",
    )(pltpu.with_memory_space_constraint(result, pltpu.VMEM))


def solution(mesh):
    placed = (
        P("member", None, "space"),
        P(),
        P(),
        P(),
        P(),
        P(),
        P(),
        P("space", None),
        P(None, "space"),
        P(("member", "space"), None, None),
        P(("member", "space"), None, None),
        P(("member", "space"), None),
    )
    return jax.shard_map(
        body, mesh=mesh, in_specs=placed, out_specs=P("member", None, "space"), check_vma=False
    )
```
